32 devices in a mesh: row: 16 (over z, x, core), col: 2 (over y).
Axes of the slice: x: 2, y: 2, z: 4, core: 2. Of those that a mesh axis runs over, the one named last changes fastest.
Arguments:
- pair_rep: bfloat16 [256, 256, 128], P('row', 'col'), may hold values from -6 to 6
- chain_len: int32 [4], replicated, may hold values from 1 to 64, as said below
- tri_gain: float32 [128], replicated, may hold values from 0.5 to 2
- tri_in: bfloat16 [128, 640], replicated, may hold values from -0.5 to 0.5
- sum_gain: float32 [128], replicated, may hold values from 0.5 to 2
- tri_out: bfloat16 [128, 128], replicated, may hold values from -0.5 to 0.5
- att_gain: float32 [128], replicated, may hold values from 0.5 to 8
- att_in: bfloat16 [128, 512], replicated, may hold values from -0.5 to 0.5
- att_bias: bfloat16 [128, 4], replicated, may hold values from -2 to 2
- att_out: bfloat16 [128, 128], replicated, may hold values from -4 to 4
Outputs:
- new_pair: bfloat16 [256, 256, 128], P('row', 'col')
The draws below stay inside these ranges and needn't reach their ends.
Inputs may be any that keep to these rules, and one draw needn't show every extreme that they name: `chain_len`: one chain in every draw has all 64 slots live.
All inputs are finite; a program needn't handle non-finite values.
Results may differ from the reference program's by a relative error of at most 0.039.
The reference program's roundings to bfloat16 on the way count: a program that leaves them out, or rounds other values in their place, can miss the bound.
Values may be sent and summed in bfloat16 or wider, within the bound.
No kernel may reach another device: no remote copies, remote signals or barrier semaphores. Data moves between devices by JAX's collectives and lax.ppermute only.
A program may use at most 128 MiB of HBM per device.

```python
import math
import jax
import jax.numpy as jnp
from jax import lax

C = 128
CH = 128
H = 4
DH = 32
TOK_ROW = 16
KCD = 16
SLOT = 64
N_TOK = 256
COLBLK = 128
KC = 32
NCHAIN = 4
HD = 128
N_COL = 2


def draw_chain_len(key, part):
    key_lengths = jax.random.fold_in(key, 11)
    key_full = jax.random.fold_in(key, 12)
    lengths = jax.random.randint(key_lengths, (NCHAIN,), 1, SLOT + 1, dtype=jnp.int32)
    full_chain = jax.random.randint(key_full, (), 0, NCHAIN, dtype=jnp.int32)
    return lengths.at[full_chain].set(SLOT)


def draw_att_gain(key, part):
    return jax.random.uniform(key, (C,), jnp.float32, 0.5, 2.0)


def block_scale(key, shape, split, smallest, top_value):
    gain = 1.0
    for axis_at, blocks in split:
        draws = jax.random.uniform(jax.random.fold_in(jax.random.fold_in(key, 6), axis_at), (blocks,), jnp.float32, smallest / len(split), top_value / len(split))
        gain = gain * jnp.repeat(jnp.exp(draws), shape[axis_at] // blocks).reshape((-1,) + (1,) * (len(shape) - 1 - axis_at))
    return gain


def normal_values(rng, shape, deviation, bound, shards=(), held_as=jnp.bfloat16):
    factor_of = block_scale(rng, shape, shards, -0.22, 0.18) if shards else 1.0
    entries = jax.random.normal(rng, shape, jnp.float32) * deviation * factor_of
    return jnp.minimum(jnp.maximum(entries, -bound), bound).astype(held_as)


def setup_inputs(seed: int = 0) -> dict:
    streams_of = jax.random.split(jax.random.key(seed), 11)
    pair_rep = normal_values(streams_of[0], (N_TOK, N_TOK, C), 1.0, 6.0, ((0, 16), (1, 2)))
    chain_len = draw_chain_len(jax.random.fold_in(streams_of[10], 71), 0)
    tri_gain = jnp.clip(jax.random.uniform(streams_of[2], (C,), jnp.float32, 0.5, 2.0), 0.5, 2.0)
    tri_in = normal_values(streams_of[3], (C, 4 * CH + C), C ** -0.5, 0.5)
    sum_gain = jnp.clip(jax.random.uniform(streams_of[4], (CH,), jnp.float32, 0.5, 2.0), 0.5, 2.0)
    tri_out = normal_values(streams_of[5], (CH, C), CH ** -0.5, 0.5)
    att_gain = draw_att_gain(jax.random.fold_in(streams_of[10], 71), 0)
    att_in = normal_values(streams_of[7], (C, 4 * HD), C ** -0.5, 0.5)
    att_bias = normal_values(streams_of[8], (C, H), (max(1, C // 16)) ** -0.5, 2.0)
    att_out = normal_values(streams_of[9], (HD, C), (max(1, H * DH // 64)) ** -0.5, 4.0)
    return {"pair_rep": pair_rep, "chain_len": chain_len, "tri_gain": tri_gain, "tri_in": tri_in, "sum_gain": sum_gain, "tri_out": tri_out, "att_gain": att_gain, "att_in": att_in, "att_bias": att_bias, "att_out": att_out}


EPSILON = 1e-05
NEG_SCORE = -1e+30

def layer_norm(values, norm_gain):
    values = values.astype(jnp.float32)
    centre = values - lax.optimization_barrier(jnp.mean(values, axis=-1, keepdims=True))
    spread = lax.optimization_barrier(jnp.mean(centre * centre, axis=-1, keepdims=True))
    return centre * lax.rsqrt(spread + EPSILON) * norm_gain

def reference(pair_rep, chain_len, tri_gain, tri_in, sum_gain, tri_out, att_gain, att_in, att_bias, att_out):
    positions = lax.broadcasted_iota(jnp.int32, (NCHAIN, SLOT), 1)
    live_mask = (positions < chain_len[:, None]).astype(jnp.float32).reshape(N_TOK)
    group_pair = pair_rep.reshape(N_TOK, N_COL, COLBLK, C)[:, :, :KCD].reshape(N_TOK, KC, C)
    group_live = live_mask.reshape(N_COL, COLBLK)[:, :KCD].reshape(KC)
    group_norm = layer_norm(group_pair, tri_gain).astype(jnp.bfloat16)
    group_proj = jnp.dot(group_norm, tri_in[:, :4 * CH], preferred_element_type=jnp.float32)
    pair_live = live_mask[:, None, None] * group_live[None, :, None]
    left_edge = (jax.nn.sigmoid(group_proj[..., :CH]) * group_proj[..., CH:2 * CH] * pair_live).astype(jnp.bfloat16)
    right_edge = (jax.nn.sigmoid(group_proj[..., 2 * CH:3 * CH]) * group_proj[..., 3 * CH:4 * CH] * pair_live).astype(jnp.bfloat16)
    right_wide = right_edge.astype(jnp.float32)
    starts = jnp.arange(N_TOK // TOK_ROW, dtype=jnp.int32) * TOK_ROW

    def triangle_block(row_first):
        rows_pair = lax.dynamic_slice_in_dim(pair_rep, row_first, TOK_ROW, 0)
        rows_left = lax.dynamic_slice_in_dim(left_edge, row_first, TOK_ROW, 0)
        rows_norm = layer_norm(rows_pair, tri_gain).astype(jnp.bfloat16)
        out_gate = jax.nn.sigmoid(jnp.dot(rows_norm, tri_in[:, 4 * CH:], preferred_element_type=jnp.float32))
        tri_sum = jnp.einsum('ikc,jkc->ijc', rows_left.astype(jnp.float32), right_wide, precision=lax.Precision.HIGHEST)
        sum_norm = layer_norm(tri_sum, sum_gain).astype(jnp.bfloat16)
        update = jnp.dot(sum_norm, tri_out, preferred_element_type=jnp.float32)
        return (rows_pair.astype(jnp.float32) + out_gate * update).astype(jnp.bfloat16)
    mid_pair = lax.map(triangle_block, starts).reshape(N_TOK, N_TOK, C)

    def bias_block(row_first):
        rows_pair = lax.dynamic_slice_in_dim(mid_pair, row_first, TOK_ROW, 0)
        rows_norm = layer_norm(rows_pair, att_gain).astype(jnp.bfloat16)
        return jnp.dot(rows_norm, att_bias, preferred_element_type=jnp.float32).astype(jnp.bfloat16)
    pair_bias = jnp.transpose(lax.map(bias_block, starts).reshape(N_TOK, N_TOK, H), (2, 0, 1))
    key_mask = live_mask > 0.5

    def attend_row(row_pair):
        row_norm = layer_norm(row_pair, att_gain).astype(jnp.bfloat16)
        projected = jnp.dot(row_norm, att_in, preferred_element_type=jnp.float32)
        queries = projected[:, :HD].astype(jnp.bfloat16).reshape(N_TOK, H, DH)
        keys = projected[:, HD:2 * HD].astype(jnp.bfloat16).reshape(N_TOK, H, DH)
        values = projected[:, 2 * HD:3 * HD].astype(jnp.bfloat16).reshape(N_TOK, H, DH)
        att_gate = jax.nn.sigmoid(projected[:, 3 * HD:])
        scores = jnp.einsum('jhd,khd->hjk', queries.astype(jnp.float32), keys.astype(jnp.float32), precision=lax.Precision.HIGHEST) / math.sqrt(DH) + pair_bias
        scores = jnp.where(key_mask[None, None, :], scores, NEG_SCORE)
        row_top = lax.optimization_barrier(jnp.max(scores, axis=-1, keepdims=True))
        weights = jnp.exp(scores - row_top).astype(jnp.bfloat16)
        totals = lax.optimization_barrier(jnp.sum(weights.astype(jnp.float32), axis=-1))
        summed = jnp.einsum('hjk,khd->jhd', weights.astype(jnp.float32), values.astype(jnp.float32), precision=lax.Precision.HIGHEST)
        attended = summed / jnp.transpose(totals)[:, :, None]
        attended = (attended.reshape(N_TOK, HD) * att_gate).astype(jnp.bfloat16)
        return (row_pair.astype(jnp.float32) + jnp.dot(attended, att_out, preferred_element_type=jnp.float32)).astype(jnp.bfloat16)
    return lax.map(attend_row, mid_pair)
```

```python
import math

import jax
import jax.numpy as jnp
from jax import lax
from jax.experimental import pallas as pl
from jax.experimental.pallas import tpu as pltpu
from jax.sharding import PartitionSpec as P

CH = 128
H = 4
DH = 32
KCD = 16
SLOT = 64

EPSILON = 1e-05
NEG_SCORE = -1e30
LOG2E = 1.4426950408889634
VMEM_LIMIT = 60 * 1024 * 1024

F32 = jnp.float32
BF16 = jnp.bfloat16


def layer_norm(values, norm_gain):
    centre = values - jnp.mean(values, axis=-1, keepdims=True)
    spread = jnp.mean(centre * centre, axis=-1, keepdims=True)
    return centre * lax.rsqrt(spread + EPSILON) * norm_gain


def sigmoid(values):
    return jax.nn.sigmoid(values)


def dot(a, b):
    return jnp.dot(a, b, preferred_element_type=F32)


def dot_nt(a, b):
    return lax.dot_general(a, b, (((1,), (1,)), ((), ())), preferred_element_type=F32)


def call(kernel, name, out_shape, n_smem, n_in, scratch=()):
    smem = pl.BlockSpec(memory_space=pltpu.SMEM)
    vmem = pl.BlockSpec(memory_space=pltpu.VMEM)
    outs = jax.tree.map(lambda _: vmem, out_shape)
    return pl.pallas_call(
        kernel,
        name=name,
        out_shape=out_shape,
        in_specs=[smem] * n_smem + [vmem] * n_in,
        out_specs=outs,
        scratch_shapes=list(scratch),
        compiler_params=pltpu.CompilerParams(vmem_limit_bytes=VMEM_LIMIT),
    )


def edge_kernel(len_ref, pair_ref, gain_ref, w_ref, out_ref, scratch_ref):
    rows, kcd, width = pair_ref.shape
    row_start = lax.axis_index("row") * rows
    cells = rows * kcd
    normed = layer_norm(pair_ref[...].reshape(cells, width).astype(F32), gain_ref[...])
    proj = dot(normed.astype(BF16), w_ref[...])
    row_len = len_ref[row_start // SLOT]
    row_base = row_start % SLOT
    col_len = len_ref[len_ref.shape[0] - 1]
    cell = lax.broadcasted_iota(jnp.int32, (cells, width), 0)
    row_live = (cell // kcd + row_base) < row_len
    live = jnp.where(row_live & (cell % kcd < col_len), 1.0, 0.0).astype(F32)
    left = sigmoid(proj[:, :CH]) * proj[:, CH : 2 * CH] * live
    right = sigmoid(proj[:, 2 * CH : 3 * CH]) * proj[:, 3 * CH : 4 * CH] * live
    out_ref[0] = left.astype(BF16).reshape(rows, kcd, width)
    scratch_ref[...] = right
    for k in range(kcd):
        out_ref[1, k] = scratch_ref[pl.ds(k, rows, stride=kcd), :].astype(BF16)


def gate_kernel(pair_ref, gain_ref, w_ref, out_ref):
    rows, cols, width = pair_ref.shape
    step = 2

    def body(t, carry):
        at = pl.ds(t * step, step)
        x = pair_ref[at].reshape(step * cols, width).astype(F32)
        normed = layer_norm(x, gain_ref[...]).astype(BF16)
        out_ref[at] = sigmoid(dot(normed, w_ref[...])).reshape(step, cols, width)
        return carry

    lax.fori_loop(0, rows // step, body, 0)


def make_tri_kernel(n_col, n_blk, place):
    def kernel(*refs):
        lefts = refs[:n_col]
        rights = refs[n_col : n_col + n_blk]
        (pair_ref, gate_ref, sum_gain_ref, w_ref, att_gain_ref, bias_w_ref) = refs[
            n_col + n_blk : n_col + n_blk + 6
        ]
        mid_ref, norm_ref, bias_ref, left_ref, sum_ref, bias_scr = refs[n_col + n_blk + 6 :]
        rows, cols, width = pair_ref.shape
        kcd = lefts[0].shape[2]
        blk = rights[0].shape[2]
        for d in range(n_col):
            left_ref[d] = lefts[d][0].reshape(rows * kcd, width).astype(F32)
        group = 8
        for s in range(n_blk):
            first = pl.multiple_of(place(s) * blk, blk)

            def sums(g, carry, s=s, first=first):
                acc = [jnp.zeros((blk, width), F32) for _ in range(group)]
                for d in range(n_col):
                    for k in range(kcd):
                        right = rights[s][d, k].astype(F32)
                        for u in range(group):
                            left = left_ref[d, pl.ds((g * group + u) * kcd + k, 1), :]
                            acc[u] = acc[u] + left * right
                for u in range(group):
                    sum_ref[g * group + u, pl.ds(first, blk), :] = acc[u]
                return carry

            lax.fori_loop(0, rows // group, sums, 0)
        step = 2

        def finish(t, carry):
            at = pl.ds(t * step, step)
            total = sum_ref[at].reshape(step * cols, width)
            normed = layer_norm(total, sum_gain_ref[...]).astype(BF16)
            update = dot(normed, w_ref[...])
            pair = pair_ref[at].reshape(step * cols, width).astype(F32)
            gate = gate_ref[at].reshape(step * cols, width)
            mid = (pair + gate * update).astype(BF16)
            mid_ref[at] = mid.reshape(step, cols, width)
            att = layer_norm(mid.astype(F32), att_gain_ref[...]).astype(BF16)
            norm_ref[at] = att.reshape(step, cols, width)
            bias = dot_nt(bias_w_ref[...], att)
            for u in range(step):
                bias_scr[t * step + u] = bias[:, u * cols : (u + 1) * cols]
            return carry

        lax.fori_loop(0, rows // step, finish, 0)
        for h in range(H):
            bias_ref[h] = bias_scr[:, h, :].astype(BF16)

    return kernel


def project_kernel(norm_ref, w_ref, q_ref, k_ref, v_ref, gate_ref):
    rows, cols, width = norm_ref.shape
    step = 2

    def body(t, carry):
        at = pl.ds(t * step, step)
        out = dot(norm_ref[at].reshape(step * cols, width), w_ref[...])
        shape = (step, cols, width)
        q_ref[at] = out[:, :width].astype(BF16).reshape(shape)
        k_ref[at] = out[:, width : 2 * width].astype(BF16).reshape(shape)
        v_ref[at] = out[:, 2 * width : 3 * width].astype(BF16).reshape(shape)
        gate_ref[at] = sigmoid(out[:, 3 * width :]).reshape(shape)
        return carry

    lax.fori_loop(0, rows // step, body, 0)


def make_attend_kernel(n_col, n_blk, place, col_of):
    def kernel(*refs):
        len_ref = refs[0]
        biases = refs[1 : 1 + n_blk]
        others = refs[1 + n_blk : n_blk + n_col]
        q_ref, k_ref, v_ref, gate_ref, mid_ref, gain_ref, kv_w_ref, out_w_ref = refs[
            n_blk + n_col : n_blk + n_col + 8
        ]
        out_ref, bias_ref = refs[n_blk + n_col + 8 :]
        rows, cols, width = q_ref.shape
        blk = biases[0].shape[2]
        chains = cols // SLOT
        lane = lax.broadcasted_iota(jnp.int32, (blk, cols), 1)
        for d in range(n_col):
            first_chain = col_of(d) * chains
            limit = jnp.zeros((blk, cols), jnp.int32)
            for q in range(chains):
                inside = lane // SLOT == q
                limit = jnp.where(inside, q * SLOT + len_ref[first_chain + q], limit)
            live = lane < limit
            for s in range(n_blk):
                first = place(s) * blk
                for h in range(H):
                    at = pl.multiple_of(h * cols + first, blk)
                    value = biases[s][d, h].astype(F32) * LOG2E
                    bias_ref[pl.ds(at, blk), d * cols : (d + 1) * cols] = jnp.where(
                        live, value, NEG_SCORE
                    )
        head = lax.broadcasted_iota(jnp.int32, (cols, width), 1) // DH
        scale = LOG2E / math.sqrt(DH)
        ones = jnp.ones((n_col * cols, width), BF16)

        def attend(i, carry):
            keys = [k_ref[i]]
            values = [v_ref[i]]
            for d in range(n_col - 1):
                normed = layer_norm(others[d][i].astype(F32), gain_ref[...]).astype(BF16)
                kv = dot(normed, kv_w_ref[...]).astype(BF16)
                keys.append(kv[:, :width])
                values.append(kv[:, width:])
            key = jnp.concatenate(keys, axis=0)
            value = jnp.concatenate([jnp.concatenate(values, axis=0), ones], axis=1)
            query = q_ref[i]
            summed = jnp.zeros((cols, width), F32)
            totals = jnp.ones((cols, width), F32)
            for h in range(H):
                mine = head == h
                scores = dot_nt(jnp.where(mine, query, jnp.zeros_like(query)), key)
                scores = scores * scale + bias_ref[pl.ds(h * cols, cols), :]
                top = jnp.max(scores, axis=-1, keepdims=True)
                weights = jnp.exp2(scores - top).astype(BF16)
                both = dot(weights, value)
                summed = jnp.where(mine, both[:, :width], summed)
                totals = jnp.where(mine, both[:, width:], totals)
            attended = (summed / totals * gate_ref[i]).astype(BF16)
            new = mid_ref[i].astype(F32) + dot(attended, out_w_ref[...])
            out_ref[i] = new.astype(BF16)
            return carry

        lax.fori_loop(0, rows, attend, 0)

    return kernel


class Grid:
    def __init__(self, n_row, n_col):
        self.n_row = n_row
        self.n_col = n_col
        self.n_blk = n_row // n_col
        self.fast = n_col == 2 and n_row & (n_row - 1) == 0
        self.offsets = [0]
        if self.fast:
            bit = self.n_blk // 2
            while bit:
                self.offsets = self.offsets + [o ^ bit for o in self.offsets]
                bit //= 2

    def place(self, s):
        if self.fast:
            return (lax.axis_index("row") & (self.n_blk - 1)) ^ self.offsets[s]
        return s

    def col_of(self, d):
        return (lax.axis_index("col") + d) % self.n_col

    def move(self, value, target):
        pairs = []
        for r in range(self.n_row):
            for c in range(self.n_col):
                to_r, to_c = target(r, c)
                pairs.append((r * self.n_col + c, to_r * self.n_col + to_c))
        return lax.ppermute(value, ("row", "col"), pairs)

    def shift_col(self, value, d):
        return self.move(value, lambda r, c: (r, (c - d) % self.n_col))

    def flip_row(self, value, bit):
        return self.move(value, lambda r, c: (r ^ bit, c))

    def gather(self, own, across):
        if not self.fast:
            stacked = lax.all_gather(own, "row", axis=0)
            stacked = lax.all_to_all(stacked, "col", split_axis=0, concat_axis=0, tiled=True)
            stacked = stacked.reshape((self.n_col, self.n_blk) + own.shape)
            order = (lax.axis_index("col") + jnp.arange(self.n_col)) % self.n_col
            stacked = jnp.take(stacked, order, axis=0)
            return [stacked[:, s] for s in range(self.n_blk)]
        half = self.n_row // 2
        same = lax.axis_index("row") // half == lax.axis_index("col")
        far = self.flip_row(own, half)
        far_across = self.shift_col(far, 1)
        pair = jnp.where(same, jnp.stack([own, across]), jnp.stack([far, far_across]))
        blocks = [pair]
        bit = self.n_blk // 2
        while bit:
            blocks = blocks + [self.flip_row(block, bit) for block in blocks]
            bit //= 2
        return blocks


def make_body(grid):
    def body(
        pair_rep, chain_len, tri_gain, tri_in, sum_gain, tri_out, att_gain, att_in, att_bias, att_out
    ):
        rows, cols, width = pair_rep.shape
        n_col, n_blk = grid.n_col, grid.n_blk
        whole = (rows, cols, width)
        tri_gain = tri_gain.reshape(1, width)
        sum_gain = sum_gain.reshape(1, width)
        att_gain = att_gain.reshape(1, width)
        chains = cols // SLOT
        first_len = lax.dynamic_slice_in_dim(chain_len, lax.axis_index("col") * chains, 1)
        lens = jnp.concatenate([chain_len, first_len])

        edges = pl.pallas_call(
            edge_kernel,
            name="edges",
            grid=(1,),
            out_shape=jax.ShapeDtypeStruct((2, rows, KCD, width), BF16),
            in_specs=[
                pl.BlockSpec(memory_space=pltpu.SMEM),
                pl.BlockSpec((rows, KCD, width), lambda g: (0, 0, 0)),
                pl.BlockSpec((1, width), lambda g: (0, 0)),
                pl.BlockSpec((width, 4 * CH), lambda g: (0, 0)),
            ],
            out_specs=pl.BlockSpec((2, rows, KCD, width), lambda g: (0, 0, 0, 0)),
            scratch_shapes=[pltpu.VMEM((rows * KCD, width), F32)],
        )(lens, pair_rep, tri_gain, tri_in)

        gate = call(gate_kernel, "out_gate", jax.ShapeDtypeStruct(whole, F32), 0, 3)(
            pair_rep, tri_gain, tri_in[:, 4 * CH :]
        )
        across = [grid.shift_col(edges, d) for d in range(1, n_col)]
        rights = grid.gather(edges[1], across[0][1])
        head_rows = 16
        bias_w = jnp.zeros((head_rows, width), BF16).at[:H].set(att_bias.T)
        mid, normed, bias = call(
            make_tri_kernel(n_col, n_blk, grid.place),
            "triangle",
            (
                jax.ShapeDtypeStruct(whole, BF16),
                jax.ShapeDtypeStruct(whole, BF16),
                jax.ShapeDtypeStruct((H, rows, cols), BF16),
            ),
            0,
            n_col + n_blk + 6,
            [
                pltpu.VMEM((n_col, rows * KCD, width), F32),
                pltpu.VMEM(whole, F32),
                pltpu.VMEM((rows, head_rows, cols), F32),
            ],
        )(edges, *across, *rights, pair_rep, gate, sum_gain, tri_out, att_gain, bias_w)

        bias_across = grid.shift_col(bias, 1)
        others = [grid.shift_col(mid, d) for d in range(1, n_col)]
        biases = grid.gather(bias, bias_across)
        wide = jax.ShapeDtypeStruct(whole, BF16)
        query, key, value, att_gate = call(
            project_kernel, "project", (wide, wide, wide, jax.ShapeDtypeStruct(whole, F32)), 0, 2
        )(normed, att_in)
        hd = H * DH
        new_pair = call(
            make_attend_kernel(n_col, n_blk, grid.place, grid.col_of),
            "attend",
            wide,
            1,
            n_blk + n_col - 1 + 8,
            [pltpu.VMEM((H * cols, n_col * cols), F32)],
        )(
            chain_len,
            *biases,
            *others,
            query,
            key,
            value,
            att_gate,
            mid,
            att_gain,
            att_in[:, hd : 3 * hd],
            att_out,
        )
        return new_pair

    return body


def solution(mesh):
    grid = Grid(mesh.shape["row"], mesh.shape["col"])
    placed = (P("row", "col", None), P(), P(), P(), P(), P(), P(), P(), P(), P())
    return jax.shard_map(
        make_body(grid), mesh=mesh, in_specs=placed, out_specs=P("row", "col", None), check_vma=False
    )
```

```python
import functools
import math

import jax
import jax.numpy as jnp
from jax import lax
from jax.experimental import pallas as pl
from jax.experimental.pallas import tpu as pltpu
from jax.sharding import PartitionSpec as P


CH = 128
H = 4
DH = 32
KCD = 16
SLOT = 64

EPSILON = 1e-05
NEG_SCORE = -1e30
VMEM_LIMIT = 60 * 1024 * 1024

F32 = jnp.float32
BF16 = jnp.bfloat16


def layer_norm(values, norm_gain):
    centre = values - jnp.mean(values, axis=-1, keepdims=True)
    spread = jnp.mean(centre * centre, axis=-1, keepdims=True)
    return centre * lax.rsqrt(spread + EPSILON) * norm_gain


def sigmoid(values):
    return jax.nn.sigmoid(values)


def dot(a, b):
    return jnp.dot(a, b, preferred_element_type=F32)


def dot_nt(a, b):
    return lax.dot_general(a, b, (((1,), (1,)), ((), ())), preferred_element_type=F32)


def call(kernel, out_shape, n_smem, n_in, scratch=()):
    smem = pl.BlockSpec(memory_space=pltpu.SMEM)
    vmem = pl.BlockSpec(memory_space=pltpu.VMEM)
    outs = jax.tree.map(lambda _: vmem, out_shape)
    return pl.pallas_call(
        kernel,
        out_shape=out_shape,
        in_specs=[smem] * n_smem + [vmem] * n_in,
        out_specs=outs,
        scratch_shapes=list(scratch),
        compiler_params=pltpu.CompilerParams(vmem_limit_bytes=VMEM_LIMIT),
    )


def edge_kernel(len_ref, pair_ref, gain_ref, w_ref, left_ref, right_ref, scratch_ref, *, cols):
    rows, kcd, width = pair_ref.shape
    row_start = lax.axis_index("row") * rows
    col_start = lax.axis_index("col") * cols
    cells = rows * kcd
    normed = layer_norm(pair_ref[...].reshape(cells, width).astype(F32), gain_ref[...])
    proj = dot(normed.astype(BF16), w_ref[...])
    row_len = len_ref[row_start // SLOT]
    row_base = row_start % SLOT
    col_len = len_ref[col_start // SLOT]
    cell = lax.broadcasted_iota(jnp.int32, (cells, width), 0)
    row_live = (cell // kcd + row_base) < row_len
    live = jnp.where(row_live & (cell % kcd < col_len), 1.0, 0.0).astype(F32)
    right = sigmoid(proj[:, 2 * CH : 3 * CH]) * proj[:, 3 * CH : 4 * CH] * live
    scratch_ref[...] = right
    for k in range(kcd):
        right_ref[k] = scratch_ref[pl.ds(k, rows, stride=kcd), :].astype(BF16)
    left = sigmoid(proj[:, :CH]) * proj[:, CH : 2 * CH] * live
    left_ref[...] = left.astype(BF16).reshape(rows, kcd, width)


def gate_kernel(pair_ref, gain_ref, w_ref, out_ref):
    rows, cols, width = pair_ref.shape
    step = 2

    def body(t, carry):
        at = pl.ds(t * step, step)
        x = pair_ref[at].reshape(step * cols, width).astype(F32)
        normed = layer_norm(x, gain_ref[...]).astype(BF16)
        out_ref[at] = sigmoid(dot(normed, w_ref[:, 4 * CH :])).reshape(step, cols, width)
        return carry

    lax.fori_loop(0, rows // step, body, 0, unroll=2)


def make_tri_kernel(n_col, n_blk, place):
    def kernel(*refs):
        lefts = refs[:n_col]
        rights = refs[n_col : n_col + n_blk]
        (pair_ref, gate_ref, sum_gain_ref, w_ref, att_gain_ref, bias_w_ref) = refs[
            n_col + n_blk : n_col + n_blk + 6
        ]
        mid_ref, norm_ref, bias_ref, left_ref, sum_ref, bias_scr = refs[n_col + n_blk + 6 :]
        rows, cols, width = pair_ref.shape
        kcd = lefts[0].shape[1]
        blk = rights[0].shape[2]
        for d in range(n_col):
            left_ref[d] = lefts[d][...].reshape(rows * kcd, width).astype(F32)
        group = 8
        for s in range(n_blk):
            first = pl.multiple_of(place(s) * blk, blk)

            def sums(g, carry, s=s, first=first):
                acc = [jnp.zeros((blk, width), F32) for _ in range(group)]
                for d in range(n_col):
                    for k in range(kcd):
                        right = rights[s][d, k].astype(F32)
                        for u in range(group):
                            left = left_ref[d, pl.ds((g * group + u) * kcd + k, 1), :]
                            acc[u] = acc[u] + left * right
                for u in range(group):
                    sum_ref[g * group + u, pl.ds(first, blk), :] = acc[u]
                return carry

            lax.fori_loop(0, rows // group, sums, 0)
        step = 2

        def finish(t, carry):
            at = pl.ds(t * step, step)
            total = sum_ref[at].reshape(step * cols, width)
            normed = layer_norm(total, sum_gain_ref[...]).astype(BF16)
            update = dot(normed, w_ref[...])
            pair = pair_ref[at].reshape(step * cols, width).astype(F32)
            gate = gate_ref[at].reshape(step * cols, width)
            mid = (pair + gate * update).astype(BF16)
            mid_ref[at] = mid.reshape(step, cols, width)
            att = layer_norm(mid.astype(F32), att_gain_ref[...]).astype(BF16)
            norm_ref[at] = att.reshape(step, cols, width)
            bias = lax.dot_general(
                bias_w_ref[...], att, (((0,), (1,)), ((), ())), preferred_element_type=F32
            )
            for u in range(step):
                bias_scr[t * step + u] = bias[:, u * cols : (u + 1) * cols]
            return carry

        lax.fori_loop(0, rows // step, finish, 0, unroll=2)
        for h in range(H):
            bias_ref[h] = bias_scr[:, h, :].astype(BF16)

    return kernel


def project_kernel(norm_ref, w_ref, q_ref, k_ref, v_ref, gate_ref):
    rows, cols, width = norm_ref.shape
    step = 2

    def body(t, carry):
        at = pl.ds(t * step, step)
        out = dot(norm_ref[at].reshape(step * cols, width), w_ref[...])
        shape = (step, cols, width)
        q_ref[at] = out[:, :width].astype(BF16).reshape(shape)
        k_ref[at] = out[:, width : 2 * width].astype(BF16).reshape(shape)
        v_ref[at] = out[:, 2 * width : 3 * width].astype(BF16).reshape(shape)
        gate_ref[at] = sigmoid(out[:, 3 * width :]).reshape(shape)
        return carry

    lax.fori_loop(0, rows // step, body, 0)


def make_attend_kernel(n_col, n_blk, place, col_of):
    def kernel(*refs):
        len_ref = refs[0]
        biases = refs[1 : 1 + n_blk]
        others = refs[1 + n_blk : n_blk + n_col]
        q_ref, k_ref, v_ref, gate_ref, mid_ref, gain_ref, kv_w_ref, out_w_ref = refs[
            n_blk + n_col : n_blk + n_col + 8
        ]
        out_ref, bias_ref, keys_ref, values_ref = refs[n_blk + n_col + 8 :]
        rows, cols, width = q_ref.shape
        blk = biases[0].shape[2]
        chains = cols // SLOT
        lane = lax.broadcasted_iota(jnp.int32, (blk, cols), 1)
        for d in range(n_col):
            first_chain = col_of(d) * chains
            limit = jnp.zeros((blk, cols), jnp.int32)
            for q in range(chains):
                inside = lane // SLOT == q
                limit = jnp.where(inside, q * SLOT + len_ref[first_chain + q], limit)
            live = lane < limit
            for s in range(n_blk):
                first = place(s) * blk
                for h in range(H):
                    at = pl.multiple_of(h * cols + first, blk)
                    value = biases[s][d, h].astype(F32)
                    bias_ref[pl.ds(at, blk), d * cols : (d + 1) * cols] = jnp.where(
                        live, value, NEG_SCORE
                    )
        head = lax.broadcasted_iota(jnp.int32, (cols, width), 1) // DH
        khead = lax.broadcasted_iota(jnp.int32, (n_col * cols, width), 1) // DH
        scale = 1.0 / math.sqrt(DH)
        ones = jnp.ones((n_col * cols, width), BF16)

        step = 2

        def spread(t, carry):
            at = pl.ds(t * step, step)
            keys_ref[at, 0:cols] = k_ref[at]
            values_ref[at, 0:cols] = v_ref[at]
            for d in range(n_col - 1):
                there = others[d][at].reshape(step * cols, width).astype(F32)
                normed = layer_norm(there, gain_ref[...]).astype(BF16)
                kv = dot(normed, kv_w_ref[:, width : 3 * width]).astype(BF16)
                low = (d + 1) * cols
                keys_ref[at, low : low + cols] = kv[:, :width].reshape(step, cols, width)
                values_ref[at, low : low + cols] = kv[:, width:].reshape(step, cols, width)
            return carry

        lax.fori_loop(0, rows // step, spread, 0, unroll=2)

        def attend(i, carry):
            key = keys_ref[i]
            value = jnp.concatenate([values_ref[i], ones], axis=1)
            query = q_ref[i]
            stack = jnp.concatenate(
                [jnp.where(head == h, query, jnp.zeros_like(query)) for h in range(H)], axis=0
            )
            scores = dot_nt(stack, key) * scale + bias_ref[...]
            top = jnp.max(scores, axis=-1, keepdims=True)
            weights = jnp.exp(scores - top).astype(BF16)
            both = dot(weights, value)
            summed = both[:cols, :width]
            totals = both[:cols, width:]
            for h in range(1, H):
                mine = head == h
                part = both[h * cols : (h + 1) * cols]
                summed = jnp.where(mine, part[:, :width], summed)
                totals = jnp.where(mine, part[:, width:], totals)
            attended = (summed / totals * gate_ref[i]).astype(BF16)
            new = mid_ref[i].astype(F32) + dot(attended, out_w_ref[...])
            out_ref[i] = new.astype(BF16)
            return carry

        lax.fori_loop(0, rows, attend, 0, unroll=4)

    return kernel


class Grid:
    def __init__(self, n_row, n_col):
        self.n_row = n_row
        self.n_col = n_col
        self.n_blk = n_row // n_col
        self.fast = n_col == 2 and n_row & (n_row - 1) == 0
        self.offsets = [0]
        if self.fast:
            bit = self.n_blk // 2
            while bit:
                self.offsets = self.offsets + [o ^ bit for o in self.offsets]
                bit //= 2

    def place(self, s):
        if self.fast:
            return (lax.axis_index("row") & (self.n_blk - 1)) ^ self.offsets[s]
        return s

    def col_of(self, d):
        return (lax.axis_index("col") + d) % self.n_col

    def move(self, value, target):
        pairs = []
        for r in range(self.n_row):
            for c in range(self.n_col):
                to = target(r, c)
                if to is not None:
                    pairs.append((r * self.n_col + c, to[0] * self.n_col + to[1]))
        return lax.ppermute(value, ("row", "col"), pairs)

    def shift_col(self, value, d):
        return self.move(value, lambda r, c: (r, (c - d) % self.n_col))

    def flip_row(self, value, bit):
        return self.move(value, lambda r, c: (r ^ bit, c))

    def gather(self, own):
        if not self.fast:
            stacked = lax.all_gather(own, "row", axis=0)
            stacked = lax.all_to_all(stacked, "col", split_axis=0, concat_axis=0, tiled=True)
            stacked = stacked.reshape((self.n_col, self.n_blk) + own.shape)
            order = (lax.axis_index("col") + jnp.arange(self.n_col)) % self.n_col
            stacked = jnp.take(stacked, order, axis=0)
            return [stacked[:, s] for s in range(self.n_blk)]
        half = self.n_row // 2
        same = lax.axis_index("row") // half == lax.axis_index("col")

        def first(r, c):
            return (r ^ half, c) if r // half == c else (r, 1 - c)

        def second(r, c):
            return None if r // half == c else (r ^ half, 1 - c)

        near = self.move(own, first)
        far = self.move(own, second)
        pair = jnp.where(same, jnp.stack([own, near]), jnp.stack([near, far]))
        blocks = [pair]
        bit = self.n_blk // 2
        while bit:
            moved = []
            for block in blocks:
                moved.append(self.flip_row(block, bit))
            blocks = blocks + moved
            bit //= 2
        return blocks


def make_body(grid):
    def body(
        pair_rep, chain_len, tri_gain, tri_in, sum_gain, tri_out, att_gain, att_in, att_bias, att_out
    ):
        rows, cols, width = pair_rep.shape
        n_col, n_blk = grid.n_col, grid.n_blk
        whole = (rows, cols, width)
        tri_gain = tri_gain.reshape(1, width)
        sum_gain = sum_gain.reshape(1, width)
        att_gain = att_gain.reshape(1, width)

        left, right = pl.pallas_call(
            functools.partial(edge_kernel, cols=cols),
            name="edges",
            grid=(1,),
            out_shape=(
                jax.ShapeDtypeStruct((rows, KCD, width), BF16),
                jax.ShapeDtypeStruct((KCD, rows, width), BF16),
            ),
            in_specs=[
                pl.BlockSpec(memory_space=pltpu.SMEM),
                pl.BlockSpec((rows, KCD, width), lambda g: (0, 0, 0)),
                pl.BlockSpec((1, width), lambda g: (0, 0)),
                pl.BlockSpec((width, 4 * CH), lambda g: (0, 0)),
            ],
            out_specs=(
                pl.BlockSpec((rows, KCD, width), lambda g: (0, 0, 0)),
                pl.BlockSpec((KCD, rows, width), lambda g: (0, 0, 0)),
            ),
            scratch_shapes=[pltpu.VMEM((rows * KCD, width), F32)],
        )(chain_len, pair_rep, tri_gain, tri_in)
        rights = grid.gather(right)
        lefts = [left] + [grid.shift_col(left, d) for d in range(1, n_col)]
        gate = call(gate_kernel, jax.ShapeDtypeStruct(whole, F32), 0, 3)(pair_rep, tri_gain, tri_in)
        mid, normed, bias = call(
            make_tri_kernel(n_col, n_blk, grid.place),
            (
                jax.ShapeDtypeStruct(whole, BF16),
                jax.ShapeDtypeStruct(whole, BF16),
                jax.ShapeDtypeStruct((H, rows, cols), BF16),
            ),
            0,
            n_col + n_blk + 6,
            [
                pltpu.VMEM((n_col, rows * KCD, width), F32),
                pltpu.VMEM(whole, F32),
                pltpu.VMEM((rows, H, cols), F32),
            ],
        )(*lefts, *rights, pair_rep, gate, sum_gain, tri_out, att_gain, att_bias)
        biases = grid.gather(bias)
        others = [grid.shift_col(mid, d) for d in range(1, n_col)]
        wide = jax.ShapeDtypeStruct(whole, BF16)
        query, key, value, att_gate = call(
            project_kernel, (wide, wide, wide, jax.ShapeDtypeStruct(whole, F32)), 0, 2
        )(normed, att_in)
        return call(
            make_attend_kernel(n_col, n_blk, grid.place, grid.col_of),
            wide,
            1,
            n_blk + n_col - 1 + 8,
            [
                pltpu.VMEM((H * cols, n_col * cols), F32),
                pltpu.VMEM((rows, n_col * cols, width), BF16),
                pltpu.VMEM((rows, n_col * cols, width), BF16),
            ],
        )(chain_len, *biases, *others, query, key, value, att_gate, mid, att_gain, att_in, att_out)

    return body


def solution(mesh):
    grid = Grid(mesh.shape["row"], mesh.shape["col"])
    placed = (P("row", "col", None), P(), P(), P(), P(), P(), P(), P(), P(), P())
    return jax.shard_map(
        make_body(grid), mesh=mesh, in_specs=placed, out_specs=P("row", "col", None), check_vma=False
    )
```

```python
import functools
import math

import jax
import jax.numpy as jnp
from jax import lax
from jax.experimental import pallas as pl
from jax.experimental.pallas import tpu as pltpu
from jax.sharding import PartitionSpec as P


CH = 128
H = 4
DH = 32
KCD = 16
SLOT = 64

EPSILON = 1e-05
NEG_SCORE = -1e30
MIB = 1024 * 1024
RESIDENT_LIMIT = 32 * MIB

F32 = jnp.float32
BF16 = jnp.bfloat16


def layer_norm(values, norm_gain):
    centre = values - jnp.mean(values, axis=-1, keepdims=True)
    spread = jnp.mean(centre * centre, axis=-1, keepdims=True)
    return centre * lax.rsqrt(spread + EPSILON) * norm_gain


def sigmoid(values):
    return jax.nn.sigmoid(values)


def dot(a, b):
    return jnp.dot(a, b, preferred_element_type=F32)


def dot_nt(a, b):
    return lax.dot_general(a, b, (((1,), (1,)), ((), ())), preferred_element_type=F32)


def call(kernel, out_shape, n_smem, n_in, limit, scratch=(), held_out=True):
    smem = pl.BlockSpec(memory_space=pltpu.SMEM)
    vmem = pl.BlockSpec(memory_space=pltpu.VMEM)
    outs = jax.tree.map(lambda _: vmem, out_shape)
    resident = limit < RESIDENT_LIMIT
    if resident and held_out:
        out_shape = jax.tree.map(lambda o: pltpu.VMEM(o.shape, o.dtype), out_shape)
    run = pl.pallas_call(
        kernel,
        out_shape=out_shape,
        in_specs=[smem] * n_smem + [vmem] * n_in,
        out_specs=outs,
        scratch_shapes=list(scratch),
        compiler_params=pltpu.CompilerParams(vmem_limit_bytes=limit),
    )

    def apply(*args):
        if not resident:
            return run(*args)
        held = [pltpu.with_memory_space_constraint(a, pltpu.VMEM) for a in args[n_smem:]]
        return run(*args[:n_smem], *held)

    return apply


def edge_kernel(len_ref, pair_ref, gain_ref, w_ref, left_ref, right_ref, scratch_ref, *, cols):
    rows, kcd, width = pair_ref.shape
    row_start = lax.axis_index("row") * rows
    col_start = lax.axis_index("col") * cols
    cells = rows * kcd
    normed = layer_norm(pair_ref[...].reshape(cells, width).astype(F32), gain_ref[...])
    proj = dot(normed.astype(BF16), w_ref[...])
    row_len = len_ref[row_start // SLOT]
    row_base = row_start % SLOT
    col_len = len_ref[col_start // SLOT]
    cell = lax.broadcasted_iota(jnp.int32, (cells, width), 0)
    row_live = (cell // kcd + row_base) < row_len
    live = jnp.where(row_live & (cell % kcd < col_len), 1.0, 0.0).astype(F32)
    right = sigmoid(proj[:, 2 * CH : 3 * CH]) * proj[:, 3 * CH : 4 * CH] * live
    scratch_ref[...] = right
    for k in range(kcd):
        right_ref[k] = scratch_ref[pl.ds(k, rows, stride=kcd), :].astype(BF16)
    left = sigmoid(proj[:, :CH]) * proj[:, CH : 2 * CH] * live
    left_ref[...] = left.astype(BF16).reshape(rows, kcd, width)


def gate_kernel(pair_ref, gain_ref, w_ref, out_ref):
    rows, cols, width = pair_ref.shape
    step = 2

    def body(t, carry):
        at = pl.ds(t * step, step)
        x = pair_ref[at].reshape(step * cols, width).astype(F32)
        normed = layer_norm(x, gain_ref[...]).astype(BF16)
        out_ref[at] = sigmoid(dot(normed, w_ref[:, 4 * CH :])).reshape(step, cols, width)
        return carry

    lax.fori_loop(0, rows // step, body, 0, unroll=2)


def make_tri_kernel(n_col, n_blk, place):
    def kernel(*refs):
        lefts = refs[:n_col]
        rights = refs[n_col : n_col + n_blk]
        (pair_ref, gate_ref, sum_gain_ref, w_ref, att_gain_ref, bias_w_ref) = refs[
            n_col + n_blk : n_col + n_blk + 6
        ]
        mid_ref, norm_ref, bias_ref, left_ref, sum_ref, bias_scr = refs[n_col + n_blk + 6 :]
        rows, cols, width = pair_ref.shape
        kcd = lefts[0].shape[1]
        blk = rights[0].shape[2]
        for d in range(n_col):
            left_ref[d] = lefts[d][...].reshape(rows * kcd, width).astype(F32)
        group = 8
        for s in range(n_blk):
            first = pl.multiple_of(place(s) * blk, blk)

            def sums(g, carry, s=s, first=first):
                acc = [jnp.zeros((blk, width), F32) for _ in range(group)]
                for d in range(n_col):
                    for k in range(kcd):
                        right = rights[s][d, k].astype(F32)
                        for u in range(group):
                            left = left_ref[d, pl.ds((g * group + u) * kcd + k, 1), :]
                            acc[u] = acc[u] + left * right
                for u in range(group):
                    sum_ref[g * group + u, pl.ds(first, blk), :] = acc[u]
                return carry

            lax.fori_loop(0, rows // group, sums, 0)
        step = 2

        def finish(t, carry):
            at = pl.ds(t * step, step)
            total = sum_ref[at].reshape(step * cols, width)
            normed = layer_norm(total, sum_gain_ref[...]).astype(BF16)
            update = dot(normed, w_ref[...])
            pair = pair_ref[at].reshape(step * cols, width).astype(F32)
            gate = gate_ref[at].reshape(step * cols, width)
            mid = (pair + gate * update).astype(BF16)
            mid_ref[at] = mid.reshape(step, cols, width)
            att = layer_norm(mid.astype(F32), att_gain_ref[...]).astype(BF16)
            norm_ref[at] = att.reshape(step, cols, width)
            bias = dot_nt(bias_w_ref[...], att)
            for u in range(step):
                bias_scr[t * step + u] = bias[:, u * cols : (u + 1) * cols]
            return carry

        lax.fori_loop(0, rows // step, finish, 0, unroll=2)
        for h in range(H):
            bias_ref[h] = bias_scr[:, h, :].astype(BF16)

    return kernel


def project_kernel(norm_ref, w_ref, q_ref, k_ref, v_ref, gate_ref):
    rows, cols, width = norm_ref.shape
    step = 2

    def body(t, carry):
        at = pl.ds(t * step, step)
        out = dot(norm_ref[at].reshape(step * cols, width), w_ref[...])
        shape = (step, cols, width)
        q_ref[at] = out[:, :width].astype(BF16).reshape(shape)
        k_ref[at] = out[:, width : 2 * width].astype(BF16).reshape(shape)
        v_ref[at] = out[:, 2 * width : 3 * width].astype(BF16).reshape(shape)
        gate_ref[at] = sigmoid(out[:, 3 * width :]).reshape(shape)
        return carry

    lax.fori_loop(0, rows // step, body, 0, unroll=2)


def make_attend_kernel(n_col, n_blk, place, col_of):
    def kernel(*refs):
        len_ref = refs[0]
        biases = refs[1 : 1 + n_blk]
        others = refs[1 + n_blk : n_blk + n_col]
        q_ref, k_ref, v_ref, gate_ref, mid_ref, gain_ref, kv_w_ref, out_w_ref = refs[
            n_blk + n_col : n_blk + n_col + 8
        ]
        out_ref, bias_ref, keys_ref, values_ref = refs[n_blk + n_col + 8 :]
        rows, cols, width = q_ref.shape
        blk = biases[0].shape[2]
        chains = cols // SLOT
        lane = lax.broadcasted_iota(jnp.int32, (blk, cols), 1)
        for d in range(n_col):
            first_chain = col_of(d) * chains
            limit = jnp.zeros((blk, cols), jnp.int32)
            for q in range(chains):
                inside = lane // SLOT == q
                limit = jnp.where(inside, q * SLOT + len_ref[first_chain + q], limit)
            live = lane < limit
            for s in range(n_blk):
                first = place(s) * blk
                for h in range(H):
                    at = pl.multiple_of(h * cols + first, blk)
                    value = biases[s][d, h].astype(F32)
                    bias_ref[pl.ds(at, blk), d * cols : (d + 1) * cols] = jnp.where(
                        live, value, NEG_SCORE
                    )
        head = lax.broadcasted_iota(jnp.int32, (cols, width), 1) // DH
        khead = lax.broadcasted_iota(jnp.int32, (n_col * cols, width), 1) // DH
        scale = 1.0 / math.sqrt(DH)
        ones = jnp.ones((n_col * cols, width), BF16)

        step = 2

        def spread(t, carry):
            at = pl.ds(t * step, step)
            keys_ref[at, 0:cols] = k_ref[at]
            values_ref[at, 0:cols] = v_ref[at]
            for d in range(n_col - 1):
                there = others[d][at].reshape(step * cols, width).astype(F32)
                normed = layer_norm(there, gain_ref[...]).astype(BF16)
                kv = dot(normed, kv_w_ref[:, width : 3 * width]).astype(BF16)
                low = (d + 1) * cols
                keys_ref[at, low : low + cols] = kv[:, :width].reshape(step, cols, width)
                values_ref[at, low : low + cols] = kv[:, width:].reshape(step, cols, width)
            return carry

        lax.fori_loop(0, rows // step, spread, 0, unroll=2)

        def attend(i, carry):
            key = keys_ref[i]
            value = jnp.concatenate([values_ref[i], ones], axis=1)
            query = q_ref[i]
            stack = jnp.concatenate(
                [jnp.where(head == h, query, jnp.zeros_like(query)) for h in range(H)], axis=0
            )
            scores = dot_nt(stack, key) * scale + bias_ref[...]
            top = jnp.max(scores, axis=-1, keepdims=True)
            weights = jnp.exp(scores - top).astype(BF16)
            both = dot(weights, value)
            summed = both[:cols, :width]
            totals = both[:cols, width:]
            for h in range(1, H):
                mine = head == h
                part = both[h * cols : (h + 1) * cols]
                summed = jnp.where(mine, part[:, :width], summed)
                totals = jnp.where(mine, part[:, width:], totals)
            attended = (summed / totals * gate_ref[i]).astype(BF16)
            new = mid_ref[i].astype(F32) + dot(attended, out_w_ref[...])
            out_ref[i] = new.astype(BF16)
            return carry

        lax.fori_loop(0, rows, attend, 0, unroll=4)

    return kernel


class Grid:
    def __init__(self, n_row, n_col):
        self.n_row = n_row
        self.n_col = n_col
        self.n_blk = n_row // n_col
        self.fast = n_col == 2 and n_row & (n_row - 1) == 0
        self.offsets = [0]
        if self.fast:
            bit = self.n_blk // 2
            while bit:
                self.offsets = self.offsets + [o ^ bit for o in self.offsets]
                bit //= 2

    def place(self, s):
        if self.fast:
            return (lax.axis_index("row") & (self.n_blk - 1)) ^ self.offsets[s]
        return s

    def col_of(self, d):
        return (lax.axis_index("col") + d) % self.n_col

    def move(self, value, target):
        pairs = []
        for r in range(self.n_row):
            for c in range(self.n_col):
                to = target(r, c)
                if to is not None:
                    pairs.append((r * self.n_col + c, to[0] * self.n_col + to[1]))
        return lax.ppermute(value, ("row", "col"), pairs)

    def shift_col(self, value, d):
        return self.move(value, lambda r, c: (r, (c - d) % self.n_col))

    def flip_row(self, value, bit):
        return self.move(value, lambda r, c: (r ^ bit, c))

    def gather(self, own):
        if not self.fast:
            stacked = lax.all_gather(own, "row", axis=0)
            stacked = lax.all_to_all(stacked, "col", split_axis=0, concat_axis=0, tiled=True)
            stacked = stacked.reshape((self.n_col, self.n_blk) + own.shape)
            order = (lax.axis_index("col") + jnp.arange(self.n_col)) % self.n_col
            stacked = jnp.take(stacked, order, axis=0)
            return [stacked[:, s] for s in range(self.n_blk)]
        half = self.n_row // 2
        same = lax.axis_index("row") // half == lax.axis_index("col")

        def first(r, c):
            return (r ^ half, c) if r // half == c else (r, 1 - c)

        def second(r, c):
            return None if r // half == c else (r ^ half, 1 - c)

        near = self.move(own, first)
        far = self.move(own, second)
        pair = jnp.where(same, jnp.stack([own, near]), jnp.stack([near, far]))
        blocks = [pair]
        bit = self.n_blk // 2
        while bit:
            moved = []
            for block in blocks:
                moved.append(self.flip_row(block, bit))
            blocks = blocks + moved
            bit //= 2
        return blocks


def make_body(grid):
    def body(
        pair_rep, chain_len, tri_gain, tri_in, sum_gain, tri_out, att_gain, att_in, att_bias, att_out
    ):
        rows, cols, width = pair_rep.shape
        n_col, n_blk = grid.n_col, grid.n_blk
        whole = (rows, cols, width)
        limit = min(60 * MIB, 12 * MIB + 24 * H * cols * n_col * cols * 4)
        tri_gain = tri_gain.reshape(1, width)
        sum_gain = sum_gain.reshape(1, width)
        att_gain = att_gain.reshape(1, width)

        left, right = pl.pallas_call(
            functools.partial(edge_kernel, cols=cols),
            name="edges",
            grid=(1,),
            out_shape=(
                jax.ShapeDtypeStruct((rows, KCD, width), BF16),
                jax.ShapeDtypeStruct((KCD, rows, width), BF16),
            ),
            in_specs=[
                pl.BlockSpec(memory_space=pltpu.SMEM),
                pl.BlockSpec((rows, KCD, width), lambda g: (0, 0, 0)),
                pl.BlockSpec((1, width), lambda g: (0, 0)),
                pl.BlockSpec((width, 4 * CH), lambda g: (0, 0)),
            ],
            out_specs=(
                pl.BlockSpec((rows, KCD, width), lambda g: (0, 0, 0)),
                pl.BlockSpec((KCD, rows, width), lambda g: (0, 0, 0)),
            ),
            scratch_shapes=[pltpu.VMEM((rows * KCD, width), F32)],
        )(chain_len, pair_rep, tri_gain, tri_in)
        rights = grid.gather(right)
        lefts = [left] + [grid.shift_col(left, d) for d in range(1, n_col)]
        gate = call(gate_kernel, jax.ShapeDtypeStruct(whole, F32), 0, 3, limit)(
            pair_rep, tri_gain, tri_in
        )
        mid, normed, bias = call(
            make_tri_kernel(n_col, n_blk, grid.place),
            (
                jax.ShapeDtypeStruct(whole, BF16),
                jax.ShapeDtypeStruct(whole, BF16),
                jax.ShapeDtypeStruct((H, rows, cols), BF16),
            ),
            0,
            n_col + n_blk + 6,
            limit,
            [
                pltpu.VMEM((n_col, rows * KCD, width), F32),
                pltpu.VMEM(whole, F32),
                pltpu.VMEM((rows, H, cols), F32),
            ],
        )(*lefts, *rights, pair_rep, gate, sum_gain, tri_out, att_gain, att_bias.T)
        biases = grid.gather(bias)
        others = [grid.shift_col(mid, d) for d in range(1, n_col)]
        wide = jax.ShapeDtypeStruct(whole, BF16)
        query, key, value, att_gate = call(
            project_kernel, (wide, wide, wide, jax.ShapeDtypeStruct(whole, F32)), 0, 2, limit
        )(normed, att_in)
        return call(
            make_attend_kernel(n_col, n_blk, grid.place, grid.col_of),
            wide,
            1,
            n_blk + n_col - 1 + 8,
            limit,
            [
                pltpu.VMEM((H * cols, n_col * cols), F32),
                pltpu.VMEM((rows, n_col * cols, width), BF16),
                pltpu.VMEM((rows, n_col * cols, width), BF16),
            ],
            held_out=False,
        )(chain_len, *biases, *others, query, key, value, att_gate, mid, att_gain, att_in, att_out)

    return body


def solution(mesh):
    grid = Grid(mesh.shape["row"], mesh.shape["col"])
    placed = (P("row", "col", None), P(), P(), P(), P(), P(), P(), P(), P(), P())
    return jax.shard_map(
        make_body(grid), mesh=mesh, in_specs=placed, out_specs=P("row", "col", None), check_vma=False
    )
```

```python
import math

import jax
import jax.numpy as jnp
from jax import lax
from jax.experimental import pallas as pl
from jax.experimental.pallas import tpu as pltpu
from jax.sharding import PartitionSpec as P


CH = 128
H = 4
DH = 32
KCD = 16
SLOT = 64

EPSILON = 1e-05
NEG_SCORE = -1e30
MIB = 1024 * 1024
RESIDENT_LIMIT = 32 * MIB

F32 = jnp.float32
BF16 = jnp.bfloat16


def layer_norm(values, norm_gain):
    centre = values - jnp.mean(values, axis=-1, keepdims=True)
    spread = jnp.mean(centre * centre, axis=-1, keepdims=True)
    return centre * lax.rsqrt(spread + EPSILON) * norm_gain


def sigmoid(values):
    return jax.nn.sigmoid(values)


def unroll_of(count, cols):
    return max(1, min(count, 1024 // cols))


def dot(a, b):
    return jnp.dot(a, b, preferred_element_type=F32)


def dot_nt(a, b):
    return lax.dot_general(a, b, (((1,), (1,)), ((), ())), preferred_element_type=F32)


def call(kernel, out_shape, n_smem, n_in, limit, scratch=(), held_out=True, aliases=None):
    smem = pl.BlockSpec(memory_space=pltpu.SMEM)
    vmem = pl.BlockSpec(memory_space=pltpu.VMEM)
    outs = jax.tree.map(lambda _: vmem, out_shape)
    resident = limit < RESIDENT_LIMIT
    if resident and held_out:
        out_shape = jax.tree.map(lambda o: pltpu.VMEM(o.shape, o.dtype), out_shape)
    run = pl.pallas_call(
        kernel,
        out_shape=out_shape,
        in_specs=[smem] * n_smem + [vmem] * n_in,
        out_specs=outs,
        scratch_shapes=list(scratch),
        input_output_aliases=aliases or {},
        compiler_params=pltpu.CompilerParams(vmem_limit_bytes=limit),
    )

    def apply(*args):
        if not resident:
            return run(*args)
        held = [pltpu.with_memory_space_constraint(a, pltpu.VMEM) for a in args[n_smem:]]
        return run(*args[:n_smem], *held)

    return apply


def make_edge_kernel(cols, n_col, col_of):
    def kernel(len_ref, pair_ref, gain_ref, sum_gain_ref, att_gain_ref, w_ref, *rest):
        left_ref, right_ref, gains_ref, live_ref, scratch_ref, group_ref, proj_ref, sems = rest
        rows, kcd, width = group_ref.shape
        group_copy = pltpu.make_async_copy(pair_ref.at[:, 0:kcd, :], group_ref, sems.at[0])
        proj_copy = pltpu.make_async_copy(w_ref.at[:, 0 : 4 * CH], proj_ref, sems.at[1])
        group_copy.start()
        proj_copy.start()
        row_start = lax.axis_index("row") * rows
        col_start = lax.axis_index("col") * cols
        cells = rows * kcd
        gains_ref[0:1, :] = sum_gain_ref[...]
        gains_ref[1:2, :] = att_gain_ref[...]
        gains_ref[2:3, :] = gain_ref[...]
        chains = cols // SLOT
        lane = lax.broadcasted_iota(jnp.int32, (1, cols), 1)
        for d in range(n_col):
            limit = jnp.zeros((1, cols), jnp.int32)
            for q in range(chains):
                length = len_ref[col_of(d) * chains + q]
                limit = jnp.where(lane // SLOT == q, q * SLOT + length, limit)
            live_ref[:, d * cols : (d + 1) * cols] = jnp.where(lane < limit, 1.0, 0.0).astype(F32)
        group_copy.wait()
        normed = layer_norm(group_ref[...].reshape(cells, width).astype(F32), gain_ref[...])
        proj_copy.wait()
        proj = dot(normed.astype(BF16), proj_ref[...])
        row_len = len_ref[row_start // SLOT]
        row_base = row_start % SLOT
        col_len = len_ref[col_start // SLOT]
        cell = lax.broadcasted_iota(jnp.int32, (cells, width), 0)
        row_live = (cell // kcd + row_base) < row_len
        live = jnp.where(row_live & (cell % kcd < col_len), 1.0, 0.0).astype(F32)
        right = sigmoid(proj[:, 2 * CH : 3 * CH]) * proj[:, 3 * CH : 4 * CH] * live
        scratch_ref[...] = right
        for k in range(kcd):
            right_ref[k] = scratch_ref[pl.ds(k, rows, stride=kcd), :].astype(BF16)
        left = sigmoid(proj[:, :CH]) * proj[:, CH : 2 * CH] * live
        left_ref[...] = left.astype(BF16).reshape(rows, kcd, width)

    return kernel


def gate_kernel(pair_ref, gains_ref, w_ref, out_ref):
    rows, cols, width = pair_ref.shape
    step = 2

    def body(t, carry):
        at = pl.ds(t * step, step)
        x = pair_ref[at].reshape(step * cols, width).astype(F32)
        normed = layer_norm(x, gains_ref[2:3, :]).astype(BF16)
        out_ref[at] = sigmoid(dot(normed, w_ref[:, 4 * CH :])).reshape(step, cols, width)
        return carry

    lax.fori_loop(0, rows // step, body, 0, unroll=unroll_of(rows // step, cols))


def add_sums(left_ref, lefts, rights, sum_ref, places):
    rows = sum_ref.shape[0]
    kcd, width = lefts[0].shape[1:]
    blk = rights[0].shape[2]
    group = 8
    for d, left in enumerate(lefts):
        left_ref[d] = left[...].reshape(rows * kcd, width).astype(F32)
    for right_ref, place in zip(rights, places):
        first = pl.multiple_of(place * blk, blk)

        def sums(g, carry, right_ref=right_ref, first=first):
            acc = [jnp.zeros((blk, width), F32) for _ in range(group)]
            for d in range(len(lefts)):
                for k in range(kcd):
                    right = right_ref[d, k].astype(F32)
                    for u in range(group):
                        left = left_ref[d, pl.ds((g * group + u) * kcd + k, 1), :]
                        acc[u] = acc[u] + left * right
            for u in range(group):
                sum_ref[g * group + u, pl.ds(first, blk), :] = acc[u]
            return carry

        lax.fori_loop(0, rows // group, sums, 0)


def make_sum_kernel(n_col, blocks, place):
    def kernel(*refs):
        lefts = refs[:n_col]
        rights = refs[n_col : n_col + len(blocks)]
        sum_ref, left_ref = refs[-2:]
        add_sums(left_ref, lefts, rights, sum_ref, [place(s) for s in blocks])

    return kernel


def make_tri_kernel(n_col, blocks, place):
    def kernel(*refs):
        lefts = refs[:n_col]
        rights = refs[n_col : n_col + len(blocks)]
        pair_ref, gate_ref, gains_ref, w_ref, bias_w_ref = refs[
            n_col + len(blocks) : n_col + len(blocks) + 5
        ]
        mid_ref, norm_ref, bias_ref, sum_ref, left_ref, bias_scr = refs[-6:]
        rows, cols, width = pair_ref.shape
        add_sums(left_ref, lefts, rights, sum_ref, [place(s) for s in blocks])
        step = 2

        def finish(t, carry):
            at = pl.ds(t * step, step)
            total = sum_ref[at].reshape(step * cols, width)
            normed = layer_norm(total, gains_ref[0:1, :]).astype(BF16)
            update = dot(normed, w_ref[...])
            pair = pair_ref[at].reshape(step * cols, width).astype(F32)
            gate = gate_ref[at].reshape(step * cols, width)
            mid = (pair + gate * update).astype(BF16)
            mid_ref[at] = mid.reshape(step, cols, width)
            att = layer_norm(mid.astype(F32), gains_ref[1:2, :]).astype(BF16)
            norm_ref[at] = att.reshape(step, cols, width)
            bias = dot_nt(bias_w_ref[...], att)
            for u in range(step):
                bias_scr[t * step + u] = bias[:, u * cols : (u + 1) * cols]
            return carry

        lax.fori_loop(0, rows // step, finish, 0, unroll=unroll_of(rows // step, cols))
        for h in range(H):
            bias_ref[h] = bias_scr[:, h, :].astype(BF16)

    return kernel


def project_kernel(norm_ref, w_ref, q_ref, k_ref, v_ref, gate_ref):
    rows, cols, width = norm_ref.shape
    step = 2

    def body(t, carry):
        at = pl.ds(t * step, step)
        out = dot(norm_ref[at].reshape(step * cols, width), w_ref[...])
        shape = (step, cols, width)
        q_ref[at] = out[:, :width].astype(BF16).reshape(shape)
        k_ref[at] = out[:, width : 2 * width].astype(BF16).reshape(shape)
        v_ref[at] = out[:, 2 * width : 3 * width].astype(BF16).reshape(shape)
        gate_ref[at] = sigmoid(out[:, 3 * width :]).reshape(shape)
        return carry

    lax.fori_loop(0, rows // step, body, 0, unroll=unroll_of(rows // step, cols))


def make_attend_kernel(n_col, n_blk, place):
    def kernel(*refs):
        biases = refs[:n_blk]
        others = refs[n_blk : n_blk + n_col - 1]
        q_ref, k_ref, v_ref, gate_ref, mid_ref, gains_ref, live_ref, kv_w_ref, out_w_ref = refs[
            n_blk + n_col - 1 : n_blk + n_col + 8
        ]
        out_ref, bias_ref, keys_ref, values_ref = refs[n_blk + n_col + 8 :]
        rows, cols, width = q_ref.shape
        blk = biases[0].shape[2]
        for d in range(n_col):
            live = jnp.broadcast_to(live_ref[:, d * cols : (d + 1) * cols], (blk, cols)) > 0.5
            for s in range(n_blk):
                first = place(s) * blk
                for h in range(H):
                    at = pl.multiple_of(h * cols + first, blk)
                    value = biases[s][d, h].astype(F32)
                    bias_ref[pl.ds(at, blk), d * cols : (d + 1) * cols] = jnp.where(
                        live, value, NEG_SCORE
                    )
        head = lax.broadcasted_iota(jnp.int32, (cols, width), 1) // DH
        scale = 1.0 / math.sqrt(DH)
        ones = jnp.ones((n_col * cols, width), BF16)

        step = 2

        def spread(t, carry):
            at = pl.ds(t * step, step)
            keys_ref[at, 0:cols] = k_ref[at]
            values_ref[at, 0:cols] = v_ref[at]
            for d in range(n_col - 1):
                there = others[d][at].reshape(step * cols, width).astype(F32)
                normed = layer_norm(there, gains_ref[1:2, :]).astype(BF16)
                kv = dot(normed, kv_w_ref[:, width : 3 * width]).astype(BF16)
                low = (d + 1) * cols
                keys_ref[at, low : low + cols] = kv[:, :width].reshape(step, cols, width)
                values_ref[at, low : low + cols] = kv[:, width:].reshape(step, cols, width)
            return carry

        lax.fori_loop(0, rows // step, spread, 0, unroll=unroll_of(rows // step, cols))

        def attend(i, carry):
            key = keys_ref[i]
            value = jnp.concatenate([values_ref[i], ones], axis=1)
            query = q_ref[i]
            stack = jnp.concatenate(
                [jnp.where(head == h, query, jnp.zeros_like(query)) for h in range(H)], axis=0
            )
            scores = dot_nt(stack, key) * scale + bias_ref[...]
            top = jnp.max(scores, axis=-1, keepdims=True)
            weights = jnp.exp(scores - top).astype(BF16)
            both = dot(weights, value)
            summed = both[:cols, :width]
            totals = both[:cols, width:]
            for h in range(1, H):
                mine = head == h
                part = both[h * cols : (h + 1) * cols]
                summed = jnp.where(mine, part[:, :width], summed)
                totals = jnp.where(mine, part[:, width:], totals)
            out_ref[i] = (summed / totals * gate_ref[i]).astype(BF16)
            return carry

        lax.fori_loop(0, rows, attend, 0, unroll=max(1, min(rows, 2**18 // (cols * n_col * cols))))

        def finish(t, carry):
            at = pl.ds(t * step, step)
            attended = out_ref[at].reshape(step * cols, width)
            new = mid_ref[at].reshape(step * cols, width).astype(F32) + dot(attended, out_w_ref[...])
            out_ref[at] = new.astype(BF16).reshape(step, cols, width)
            return carry

        lax.fori_loop(0, rows // step, finish, 0, unroll=unroll_of(rows // step, cols))

    return kernel


class Grid:
    def __init__(self, n_row, n_col):
        self.n_row = n_row
        self.n_col = n_col
        self.n_blk = n_row // n_col
        self.fast = n_col == 2 and n_row & (n_row - 1) == 0
        self.offsets = [0]
        if self.fast:
            bit = self.n_blk // 2
            while bit:
                self.offsets = self.offsets + [o ^ bit for o in self.offsets]
                bit //= 2

    def groups(self):
        if not self.fast or self.n_blk < 8:
            return [], list(range(self.n_blk))
        half = self.n_blk // 2
        parts = [range(half // 2), range(half // 2, half - 1), range(half - 1, half)]
        groups = [[t for s in part for t in (s, s + half)] for part in parts]
        return groups[:-1], groups[-1]

    def place(self, s):
        if self.fast:
            return (lax.axis_index("row") & (self.n_blk - 1)) ^ self.offsets[s]
        return s

    def col_of(self, d):
        return (lax.axis_index("col") + d) % self.n_col

    def move(self, value, target):
        pairs = []
        for r in range(self.n_row):
            for c in range(self.n_col):
                to = target(r, c)
                if to is not None:
                    pairs.append((r * self.n_col + c, to[0] * self.n_col + to[1]))
        return lax.ppermute(value, ("row", "col"), pairs)

    def shift_col(self, value, d):
        return self.move(value, lambda r, c: (r, (c - d) % self.n_col))

    def flip_row(self, value, bit):
        return self.move(value, lambda r, c: (r ^ bit, c))

    def gather(self, own):
        if not self.fast:
            stacked = lax.all_gather(own, "row", axis=0)
            stacked = lax.all_to_all(stacked, "col", split_axis=0, concat_axis=0, tiled=True)
            stacked = stacked.reshape((self.n_col, self.n_blk) + own.shape)
            order = (lax.axis_index("col") + jnp.arange(self.n_col)) % self.n_col
            stacked = jnp.take(stacked, order, axis=0)
            return [stacked[:, s] for s in range(self.n_blk)]
        half = self.n_row // 2
        same = lax.axis_index("row") // half == lax.axis_index("col")

        def first(r, c):
            return (r ^ half, c) if r // half == c else (r, 1 - c)

        def second(r, c):
            return None if r // half == c else (r ^ half, 1 - c)

        near = self.move(own, first)
        far = self.move(own, second)
        pair = jnp.where(same, jnp.stack([own, near]), jnp.stack([near, far]))
        blocks = [pair]
        bit = self.n_blk // 2
        while bit:
            moved = []
            for block in blocks:
                moved.append(self.flip_row(block, bit))
            blocks = blocks + moved
            bit //= 2
        return blocks


def make_body(grid):
    def body(
        pair_rep, chain_len, tri_gain, tri_in, sum_gain, tri_out, att_gain, att_in, att_bias, att_out
    ):
        rows, cols, width = pair_rep.shape
        n_col, n_blk = grid.n_col, grid.n_blk
        whole = (rows, cols, width)
        limit = min(60 * MIB, 12 * MIB + 24 * H * cols * n_col * cols * 4)
        tri_gain = tri_gain.reshape(1, width)
        sum_gain = sum_gain.reshape(1, width)
        att_gain = att_gain.reshape(1, width)

        anywhere = pl.BlockSpec(memory_space=pl.ANY)
        small = pl.BlockSpec(memory_space=pltpu.VMEM)
        held = limit < RESIDENT_LIMIT
        shape = pltpu.VMEM if held else jax.ShapeDtypeStruct
        left, right, gains, live = pl.pallas_call(
            make_edge_kernel(cols, n_col, grid.col_of),
            name="edges",
            out_shape=(
                shape((rows, KCD, width), BF16),
                shape((KCD, rows, width), BF16),
                shape((3, width), F32),
                shape((1, n_col * cols), F32),
            ),
            in_specs=[
                pl.BlockSpec(memory_space=pltpu.SMEM),
                anywhere,
                small,
                small,
                small,
                anywhere,
            ],
            out_specs=(small, small, small, small),
            scratch_shapes=[
                pltpu.VMEM((rows * KCD, width), F32),
                pltpu.VMEM((rows, KCD, width), BF16),
                pltpu.VMEM((width, 4 * CH), BF16),
                pltpu.SemaphoreType.DMA((2,)),
            ],
        )(chain_len, pair_rep, tri_gain, sum_gain, att_gain, tri_in)
        rights = grid.gather(right)
        lefts = [left] + [grid.shift_col(left, d) for d in range(1, n_col)]
        gate = call(gate_kernel, jax.ShapeDtypeStruct(whole, F32), 0, 3, limit)(
            pair_rep, gains, tri_in
        )
        early, last = grid.groups()
        left_scr = pltpu.VMEM((n_col, rows * KCD, width), F32)
        sums = []
        for blocks in early:
            sums = [
                call(
                    make_sum_kernel(n_col, blocks, grid.place),
                    jax.ShapeDtypeStruct(whole, F32),
                    0,
                    n_col + len(blocks) + len(sums),
                    limit,
                    [left_scr],
                    aliases={n_col + len(blocks): 0} if sums else {},
                )(*lefts, *[rights[s] for s in blocks], *sums)
            ]
        mid, normed, bias, _ = call(
            make_tri_kernel(n_col, last, grid.place),
            (
                jax.ShapeDtypeStruct(whole, BF16),
                jax.ShapeDtypeStruct(whole, BF16),
                jax.ShapeDtypeStruct((H, rows, cols), BF16),
                jax.ShapeDtypeStruct(whole, F32),
            ),
            0,
            n_col + len(last) + 5 + len(sums),
            limit,
            [left_scr, pltpu.VMEM((rows, H, cols), F32)],
            aliases={n_col + len(last) + 5: 3} if sums else {},
        )(*lefts, *[rights[s] for s in last], pair_rep, gate, gains, tri_out, att_bias.T, *sums)
        biases = grid.gather(bias)
        others = [grid.shift_col(mid, d) for d in range(1, n_col)]
        wide = jax.ShapeDtypeStruct(whole, BF16)
        query, key, value, att_gate = call(
            project_kernel, (wide, wide, wide, jax.ShapeDtypeStruct(whole, F32)), 0, 2, limit
        )(normed, att_in)
        return call(
            make_attend_kernel(n_col, n_blk, grid.place),
            wide,
            0,
            n_blk + n_col - 1 + 9,
            limit,
            [
                pltpu.VMEM((H * cols, n_col * cols), F32),
                pltpu.VMEM((rows, n_col * cols, width), BF16),
                pltpu.VMEM((rows, n_col * cols, width), BF16),
            ],
            held_out=False,
        )(
            *biases,
            *others,
            query,
            key,
            value,
            att_gate,
            mid,
            gains,
            live,
            att_in,
            att_out,
        )

    return body


def solution(mesh):
    grid = Grid(mesh.shape["row"], mesh.shape["col"])
    placed = (P("row", "col", None), P(), P(), P(), P(), P(), P(), P(), P(), P())
    return jax.shard_map(
        make_body(grid), mesh=mesh, in_specs=placed, out_specs=P("row", "col", None), check_vma=False
    )
```

```python
import math

import jax
import jax.numpy as jnp
from jax import lax
from jax.experimental import pallas as pl
from jax.experimental.pallas import tpu as pltpu
from jax.sharding import PartitionSpec as P


CH = 128
H = 4
DH = 32
KCD = 16
SLOT = 64

EPSILON = 1e-05
NEG_SCORE = -1e30
MIB = 1024 * 1024
RESIDENT_LIMIT = 32 * MIB

F32 = jnp.float32
BF16 = jnp.bfloat16


def layer_norm(values, norm_gain):
    centre = values - jnp.mean(values, axis=-1, keepdims=True)
    spread = jnp.mean(centre * centre, axis=-1, keepdims=True)
    return centre * lax.rsqrt(spread + EPSILON) * norm_gain


def sigmoid(values):
    return jax.nn.sigmoid(values)


def unroll_of(count, cols):
    return max(1, min(count, 1024 // cols))


def dot(a, b):
    return jnp.dot(a, b, preferred_element_type=F32)


def dot_nt(a, b):
    return lax.dot_general(a, b, (((1,), (1,)), ((), ())), preferred_element_type=F32)


def call(kernel, out_shape, n_smem, n_in, limit, scratch=(), held_out=True, aliases=None):
    smem = pl.BlockSpec(memory_space=pltpu.SMEM)
    vmem = pl.BlockSpec(memory_space=pltpu.VMEM)
    outs = jax.tree.map(lambda _: vmem, out_shape)
    resident = limit < RESIDENT_LIMIT
    if resident and held_out:
        out_shape = jax.tree.map(lambda o: pltpu.VMEM(o.shape, o.dtype), out_shape)
    run = pl.pallas_call(
        kernel,
        out_shape=out_shape,
        in_specs=[smem] * n_smem + [vmem] * n_in,
        out_specs=outs,
        scratch_shapes=list(scratch),
        input_output_aliases=aliases or {},
        compiler_params=pltpu.CompilerParams(vmem_limit_bytes=limit),
    )

    def apply(*args):
        if not resident:
            return run(*args)
        held = [pltpu.with_memory_space_constraint(a, pltpu.VMEM) for a in args[n_smem:]]
        return run(*args[:n_smem], *held)

    return apply


def make_edge_kernel(cols, n_col, col_of):
    def kernel(len_ref, pair_ref, gain_ref, sum_gain_ref, att_gain_ref, w_ref, *rest):
        left_ref, right_ref, gains_ref, live_ref, scratch_ref, group_ref, proj_ref, sems = rest
        rows, kcd, width = group_ref.shape
        group_copy = pltpu.make_async_copy(pair_ref.at[:, 0:kcd, :], group_ref, sems.at[0])
        proj_copy = pltpu.make_async_copy(w_ref.at[:, 0 : 4 * CH], proj_ref, sems.at[1])
        group_copy.start()
        proj_copy.start()
        row_start = lax.axis_index("row") * rows
        col_start = lax.axis_index("col") * cols
        cells = rows * kcd
        gains_ref[0:1, :] = sum_gain_ref[...]
        gains_ref[1:2, :] = att_gain_ref[...]
        gains_ref[2:3, :] = gain_ref[...]
        chains = cols // SLOT
        lane = lax.broadcasted_iota(jnp.int32, (1, cols), 1)
        for d in range(n_col):
            limit = jnp.zeros((1, cols), jnp.int32)
            for q in range(chains):
                length = len_ref[col_of(d) * chains + q]
                limit = jnp.where(lane // SLOT == q, q * SLOT + length, limit)
            live_ref[:, d * cols : (d + 1) * cols] = jnp.where(lane < limit, 1.0, 0.0).astype(F32)
        group_copy.wait()
        normed = layer_norm(group_ref[...].reshape(cells, width).astype(F32), gain_ref[...])
        proj_copy.wait()
        proj = dot(normed.astype(BF16), proj_ref[...])
        row_len = len_ref[row_start // SLOT]
        row_base = row_start % SLOT
        col_len = len_ref[col_start // SLOT]
        cell = lax.broadcasted_iota(jnp.int32, (cells, width), 0)
        row_live = (cell // kcd + row_base) < row_len
        live = jnp.where(row_live & (cell % kcd < col_len), 1.0, 0.0).astype(F32)
        right = sigmoid(proj[:, 2 * CH : 3 * CH]) * proj[:, 3 * CH : 4 * CH] * live
        scratch_ref[...] = right
        for k in range(kcd):
            right_ref[k] = scratch_ref[pl.ds(k, rows, stride=kcd), :].astype(BF16)
        left = sigmoid(proj[:, :CH]) * proj[:, CH : 2 * CH] * live
        left_ref[...] = left.astype(BF16).reshape(rows, kcd, width)

    return kernel


def gate_kernel(pair_ref, gains_ref, w_ref, out_ref):
    rows, cols, width = pair_ref.shape
    step = 2

    def body(t, carry):
        at = pl.ds(t * step, step)
        x = pair_ref[at].reshape(step * cols, width).astype(F32)
        normed = layer_norm(x, gains_ref[2:3, :]).astype(BF16)
        out_ref[at] = sigmoid(dot(normed, w_ref[:, 4 * CH :])).reshape(step, cols, width)
        return carry

    lax.fori_loop(0, rows // step, body, 0, unroll=unroll_of(rows // step, cols))


def add_sums(left_ref, lefts, rights, sum_ref, places):
    rows = sum_ref.shape[0]
    kcd, width = lefts[0].shape[1:]
    blk = rights[0].shape[2]
    group = 8
    for d, left in enumerate(lefts):
        left_ref[d] = left[...].reshape(rows * kcd, width).astype(F32)
    for right_ref, place in zip(rights, places):
        first = pl.multiple_of(place * blk, blk)

        def sums(g, carry, right_ref=right_ref, first=first):
            acc = [jnp.zeros((blk, width), F32) for _ in range(group)]
            for d in range(len(lefts)):
                for k in range(kcd):
                    right = right_ref[d, k].astype(F32)
                    for u in range(group):
                        left = left_ref[d, pl.ds((g * group + u) * kcd + k, 1), :]
                        acc[u] = acc[u] + left * right
            for u in range(group):
                sum_ref[g * group + u, pl.ds(first, blk), :] = acc[u]
            return carry

        lax.fori_loop(0, rows // group, sums, 0)


def make_sum_kernel(n_col, blocks, place):
    def kernel(*refs):
        lefts = refs[:n_col]
        rights = refs[n_col : n_col + len(blocks)]
        sum_ref, left_ref = refs[-2:]
        add_sums(left_ref, lefts, rights, sum_ref, [place(s) for s in blocks])

    return kernel


def make_tri_kernel(n_col, blocks, place):
    def kernel(*refs):
        lefts = refs[:n_col]
        rights = refs[n_col : n_col + len(blocks)]
        pair_ref, gate_ref, gains_ref, w_ref, bias_w_ref = refs[
            n_col + len(blocks) : n_col + len(blocks) + 5
        ]
        mid_ref, norm_ref, bias_ref, sum_ref, left_ref, bias_scr = refs[-6:]
        rows, cols, width = pair_ref.shape
        add_sums(left_ref, lefts, rights, sum_ref, [place(s) for s in blocks])
        step = 2

        def finish(t, carry):
            at = pl.ds(t * step, step)
            total = sum_ref[at].reshape(step * cols, width)
            normed = layer_norm(total, gains_ref[0:1, :]).astype(BF16)
            update = dot(normed, w_ref[...])
            pair = pair_ref[at].reshape(step * cols, width).astype(F32)
            gate = gate_ref[at].reshape(step * cols, width)
            mid = (pair + gate * update).astype(BF16)
            mid_ref[at] = mid.reshape(step, cols, width)
            att = layer_norm(mid.astype(F32), gains_ref[1:2, :]).astype(BF16)
            norm_ref[at] = att.reshape(step, cols, width)
            bias = dot_nt(bias_w_ref[...], att)
            for u in range(step):
                bias_scr[t * step + u] = bias[:, u * cols : (u + 1) * cols]
            return carry

        lax.fori_loop(0, rows // step, finish, 0, unroll=unroll_of(rows // step, cols))
        for h in range(H):
            bias_ref[h] = bias_scr[:, h, :].astype(BF16)

    return kernel


def project_kernel(norm_ref, w_ref, q_ref, k_ref, v_ref, gate_ref):
    rows, cols, width = norm_ref.shape
    step = 2

    def body(t, carry):
        at = pl.ds(t * step, step)
        out = dot(norm_ref[at].reshape(step * cols, width), w_ref[...])
        shape = (step, cols, width)
        q_ref[at] = out[:, :width].astype(BF16).reshape(shape)
        k_ref[at] = out[:, width : 2 * width].astype(BF16).reshape(shape)
        v_ref[at] = out[:, 2 * width : 3 * width].astype(BF16).reshape(shape)
        gate_ref[at] = sigmoid(out[:, 3 * width :]).reshape(shape)
        return carry

    lax.fori_loop(0, rows // step, body, 0, unroll=unroll_of(rows // step, cols))


def make_attend_kernel(n_col, n_blk, place):
    def kernel(*refs):
        biases = refs[:n_blk]
        others = refs[n_blk : n_blk + n_col - 1]
        q_ref, k_ref, v_ref, gate_ref, mid_ref, gains_ref, live_ref, kv_w_ref, out_w_ref = refs[
            n_blk + n_col - 1 : n_blk + n_col + 8
        ]
        out_ref, bias_ref, keys_ref, values_ref = refs[n_blk + n_col + 8 :]
        rows, cols, width = q_ref.shape
        blk = biases[0].shape[2]
        for d in range(n_col):
            live = jnp.broadcast_to(live_ref[:, d * cols : (d + 1) * cols], (blk, cols)) > 0.5
            for s in range(n_blk):
                first = place(s) * blk
                for h in range(H):
                    at = pl.multiple_of(h * cols + first, blk)
                    value = biases[s][d, h].astype(F32)
                    bias_ref[pl.ds(at, blk), d * cols : (d + 1) * cols] = jnp.where(
                        live, value, NEG_SCORE
                    )
        head = lax.broadcasted_iota(jnp.int32, (cols, width), 1) // DH
        scale = 1.0 / math.sqrt(DH)
        ones = jnp.ones((n_col * cols, width), BF16)

        step = 2

        def spread(t, carry):
            at = pl.ds(t * step, step)
            keys_ref[at, 0:cols] = k_ref[at]
            values_ref[at, 0:cols] = v_ref[at]
            for d in range(n_col - 1):
                there = others[d][at].reshape(step * cols, width).astype(F32)
                normed = layer_norm(there, gains_ref[1:2, :]).astype(BF16)
                kv = dot(normed, kv_w_ref[:, width : 3 * width]).astype(BF16)
                low = (d + 1) * cols
                keys_ref[at, low : low + cols] = kv[:, :width].reshape(step, cols, width)
                values_ref[at, low : low + cols] = kv[:, width:].reshape(step, cols, width)
            return carry

        lax.fori_loop(0, rows // step, spread, 0, unroll=unroll_of(rows // step, cols))

        def attend(i, carry):
            key = keys_ref[i]
            value = jnp.concatenate([values_ref[i], ones], axis=1)
            query = q_ref[i]
            stack = jnp.concatenate(
                [jnp.where(head == h, query, jnp.zeros_like(query)) for h in range(H)], axis=0
            )
            scores = dot_nt(stack, key) * scale + bias_ref[...]
            top = jnp.max(scores, axis=-1, keepdims=True)
            weights = jnp.exp(scores - top).astype(BF16)
            both = dot(weights, value)
            summed = both[:cols, :width]
            totals = both[:cols, width:]
            for h in range(1, H):
                mine = head == h
                part = both[h * cols : (h + 1) * cols]
                summed = jnp.where(mine, part[:, :width], summed)
                totals = jnp.where(mine, part[:, width:], totals)
            out_ref[i] = (summed / totals * gate_ref[i]).astype(BF16)
            return carry

        lax.fori_loop(0, rows, attend, 0, unroll=max(1, min(rows, 2**18 // (cols * n_col * cols))))

        def finish(t, carry):
            at = pl.ds(t * step, step)
            attended = out_ref[at].reshape(step * cols, width)
            new = mid_ref[at].reshape(step * cols, width).astype(F32) + dot(attended, out_w_ref[...])
            out_ref[at] = new.astype(BF16).reshape(step, cols, width)
            return carry

        lax.fori_loop(0, rows // step, finish, 0, unroll=unroll_of(rows // step, cols))

    return kernel


class Grid:
    def __init__(self, n_row, n_col):
        self.n_row = n_row
        self.n_col = n_col
        self.n_blk = n_row // n_col
        self.fast = n_col == 2 and n_row & (n_row - 1) == 0
        self.offsets = [0]
        if self.fast:
            bit = self.n_blk // 2
            while bit:
                self.offsets = self.offsets + [o ^ bit for o in self.offsets]
                bit //= 2

    def groups(self):
        if not self.fast or self.n_blk < 8:
            return [], list(range(self.n_blk))
        half = self.n_blk // 2
        parts = [range(half // 2), range(half // 2, half - 1), range(half - 1, half)]
        groups = [[t for s in part for t in (s, s + half)] for part in parts]
        return groups[:-1] + [groups[-1][:1]], groups[-1][1:]

    def place(self, s):
        if self.fast:
            return (lax.axis_index("row") & (self.n_blk - 1)) ^ self.offsets[s]
        return s

    def col_of(self, d):
        return (lax.axis_index("col") + d) % self.n_col

    def move(self, value, target):
        pairs = []
        for r in range(self.n_row):
            for c in range(self.n_col):
                to = target(r, c)
                if to is not None:
                    pairs.append((r * self.n_col + c, to[0] * self.n_col + to[1]))
        return lax.ppermute(value, ("row", "col"), pairs)

    def shift_col(self, value, d):
        return self.move(value, lambda r, c: (r, (c - d) % self.n_col))

    def flip_row(self, value, bit):
        return self.move(value, lambda r, c: (r ^ bit, c))

    def gather(self, own, relay):
        if not self.fast:
            stacked = lax.all_gather(own, "row", axis=0)
            stacked = lax.all_to_all(stacked, "col", split_axis=0, concat_axis=0, tiled=True)
            stacked = stacked.reshape((self.n_col, self.n_blk) + own.shape)
            order = (lax.axis_index("col") + jnp.arange(self.n_col)) % self.n_col
            stacked = jnp.take(stacked, order, axis=0)
            return [stacked[:, s] for s in range(self.n_blk)]
        half = self.n_row // 2
        same = lax.axis_index("row") // half == lax.axis_index("col")

        def inside(r, c):
            return r // half == c

        if relay:
            near = self.move(own, lambda r, c: None if inside(r, c) else (r, 1 - c))
            both = jnp.stack([own, near])
            far = self.move(both, lambda r, c: (r ^ half, c) if inside(r, c) else None)
            pair = jnp.where(same, both, far)
        else:

            def first(r, c):
                return (r ^ half, c) if inside(r, c) else (r, 1 - c)

            def second(r, c):
                return None if inside(r, c) else (r ^ half, 1 - c)

            near = self.move(own, first)
            far = self.move(own, second)
            pair = jnp.where(same, jnp.stack([own, near]), jnp.stack([near, far]))
        blocks = [pair]
        bit = self.n_blk // 2
        while bit:
            moved = []
            for block in blocks:
                moved.append(self.flip_row(block, bit))
            blocks = blocks + moved
            bit //= 2
        return blocks


def make_body(grid):
    def body(
        pair_rep, chain_len, tri_gain, tri_in, sum_gain, tri_out, att_gain, att_in, att_bias, att_out
    ):
        rows, cols, width = pair_rep.shape
        n_col, n_blk = grid.n_col, grid.n_blk
        whole = (rows, cols, width)
        limit = min(60 * MIB, 12 * MIB + 24 * H * cols * n_col * cols * 4)
        tri_gain = tri_gain.reshape(1, width)
        sum_gain = sum_gain.reshape(1, width)
        att_gain = att_gain.reshape(1, width)

        anywhere = pl.BlockSpec(memory_space=pl.ANY)
        small = pl.BlockSpec(memory_space=pltpu.VMEM)
        held = limit < RESIDENT_LIMIT
        shape = pltpu.VMEM if held else jax.ShapeDtypeStruct
        left, right, gains, live = pl.pallas_call(
            make_edge_kernel(cols, n_col, grid.col_of),
            name="edges",
            out_shape=(
                shape((rows, KCD, width), BF16),
                shape((KCD, rows, width), BF16),
                shape((3, width), F32),
                shape((1, n_col * cols), F32),
            ),
            in_specs=[
                pl.BlockSpec(memory_space=pltpu.SMEM),
                anywhere,
                small,
                small,
                small,
                anywhere,
            ],
            out_specs=(small, small, small, small),
            scratch_shapes=[
                pltpu.VMEM((rows * KCD, width), F32),
                pltpu.VMEM((rows, KCD, width), BF16),
                pltpu.VMEM((width, 4 * CH), BF16),
                pltpu.SemaphoreType.DMA((2,)),
            ],
        )(chain_len, pair_rep, tri_gain, sum_gain, att_gain, tri_in)
        rights = grid.gather(right, False)
        lefts = [left] + [grid.shift_col(left, d) for d in range(1, n_col)]
        gate = call(gate_kernel, jax.ShapeDtypeStruct(whole, F32), 0, 3, limit)(
            pair_rep, gains, tri_in
        )
        early, last = grid.groups()
        left_scr = pltpu.VMEM((n_col, rows * KCD, width), F32)
        sums = []
        for blocks in early:
            sums = [
                call(
                    make_sum_kernel(n_col, blocks, grid.place),
                    jax.ShapeDtypeStruct(whole, F32),
                    0,
                    n_col + len(blocks) + len(sums),
                    limit,
                    [left_scr],
                    aliases={n_col + len(blocks): 0} if sums else {},
                )(*lefts, *[rights[s] for s in blocks], *sums)
            ]
        mid, normed, bias, _ = call(
            make_tri_kernel(n_col, last, grid.place),
            (
                jax.ShapeDtypeStruct(whole, BF16),
                jax.ShapeDtypeStruct(whole, BF16),
                jax.ShapeDtypeStruct((H, rows, cols), BF16),
                jax.ShapeDtypeStruct(whole, F32),
            ),
            0,
            n_col + len(last) + 5 + len(sums),
            limit,
            [left_scr, pltpu.VMEM((rows, H, cols), F32)],
            aliases={n_col + len(last) + 5: 3} if sums else {},
        )(*lefts, *[rights[s] for s in last], pair_rep, gate, gains, tri_out, att_bias.T, *sums)
        biases = grid.gather(bias, True)
        others = [grid.shift_col(mid, d) for d in range(1, n_col)]
        wide = jax.ShapeDtypeStruct(whole, BF16)
        query, key, value, att_gate = call(
            project_kernel, (wide, wide, wide, jax.ShapeDtypeStruct(whole, F32)), 0, 2, limit
        )(normed, att_in)
        return call(
            make_attend_kernel(n_col, n_blk, grid.place),
            wide,
            0,
            n_blk + n_col - 1 + 9,
            limit,
            [
                pltpu.VMEM((H * cols, n_col * cols), F32),
                pltpu.VMEM((rows, n_col * cols, width), BF16),
                pltpu.VMEM((rows, n_col * cols, width), BF16),
            ],
            held_out=False,
        )(
            *biases,
            *others,
            query,
            key,
            value,
            att_gate,
            mid,
            gains,
            live,
            att_in,
            att_out,
        )

    return body


def solution(mesh):
    grid = Grid(mesh.shape["row"], mesh.shape["col"])
    placed = (P("row", "col", None), P(), P(), P(), P(), P(), P(), P(), P(), P())
    return jax.shard_map(
        make_body(grid), mesh=mesh, in_specs=placed, out_specs=P("row", "col", None), check_vma=False
    )
```

```python
import math

import jax
import jax.numpy as jnp
from jax import lax
from jax.experimental import pallas as pl
from jax.experimental.pallas import tpu as pltpu
from jax.sharding import PartitionSpec as P


CH = 128
H = 4
DH = 32
KCD = 16
SLOT = 64

EPSILON = 1e-05
NEG_SCORE = -1e30
MIB = 1024 * 1024
RESIDENT_LIMIT = 32 * MIB

F32 = jnp.float32
BF16 = jnp.bfloat16


def layer_norm(values, norm_gain):
    centre = values - jnp.mean(values, axis=-1, keepdims=True)
    spread = jnp.mean(centre * centre, axis=-1, keepdims=True)
    return centre * lax.rsqrt(spread + EPSILON) * norm_gain


def sigmoid(values):
    return jax.nn.sigmoid(values)


def unroll_of(count, cols):
    return max(1, min(count, 1024 // cols))


def dot(a, b):
    return jnp.dot(a, b, preferred_element_type=F32)


def dot_nt(a, b):
    return lax.dot_general(a, b, (((1,), (1,)), ((), ())), preferred_element_type=F32)


def call(kernel, out_shape, n_smem, n_in, limit, scratch=(), held_out=True, aliases=None):
    smem = pl.BlockSpec(memory_space=pltpu.SMEM)
    vmem = pl.BlockSpec(memory_space=pltpu.VMEM)
    outs = jax.tree.map(lambda _: vmem, out_shape)
    resident = limit < RESIDENT_LIMIT
    if resident and held_out:
        out_shape = jax.tree.map(lambda o: pltpu.VMEM(o.shape, o.dtype), out_shape)
    run = pl.pallas_call(
        kernel,
        out_shape=out_shape,
        in_specs=[smem] * n_smem + [vmem] * n_in,
        out_specs=outs,
        scratch_shapes=list(scratch),
        input_output_aliases=aliases or {},
        compiler_params=pltpu.CompilerParams(vmem_limit_bytes=limit),
    )

    def apply(*args):
        if not resident:
            return run(*args)
        held = [pltpu.with_memory_space_constraint(a, pltpu.VMEM) for a in args[n_smem:]]
        return run(*args[:n_smem], *held)

    return apply


def make_edge_kernel(cols, n_col, col_of):
    def kernel(len_ref, pair_ref, gain_ref, sum_gain_ref, att_gain_ref, w_ref, *rest):
        left_ref, right_ref, gains_ref, live_ref, scratch_ref, group_ref, proj_ref, sems = rest
        rows, kcd, width = group_ref.shape
        group_copy = pltpu.make_async_copy(pair_ref.at[:, 0:kcd, :], group_ref, sems.at[0])
        proj_copy = pltpu.make_async_copy(w_ref.at[:, 0 : 4 * CH], proj_ref, sems.at[1])
        group_copy.start()
        proj_copy.start()
        row_start = lax.axis_index("row") * rows
        col_start = lax.axis_index("col") * cols
        cells = rows * kcd
        gains_ref[0:1, :] = sum_gain_ref[...]
        gains_ref[1:2, :] = att_gain_ref[...]
        gains_ref[2:3, :] = gain_ref[...]
        chains = cols // SLOT
        lane = lax.broadcasted_iota(jnp.int32, (1, cols), 1)
        for d in range(n_col):
            limit = jnp.zeros((1, cols), jnp.int32)
            for q in range(chains):
                length = len_ref[col_of(d) * chains + q]
                limit = jnp.where(lane // SLOT == q, q * SLOT + length, limit)
            live_ref[:, d * cols : (d + 1) * cols] = jnp.where(lane < limit, 1.0, 0.0).astype(F32)
        group_copy.wait()
        normed = layer_norm(group_ref[...].reshape(cells, width).astype(F32), gain_ref[...])
        proj_copy.wait()
        proj = dot(normed.astype(BF16), proj_ref[...])
        row_len = len_ref[row_start // SLOT]
        row_base = row_start % SLOT
        col_len = len_ref[col_start // SLOT]
        cell = lax.broadcasted_iota(jnp.int32, (cells, width), 0)
        row_live = (cell // kcd + row_base) < row_len
        live = jnp.where(row_live & (cell % kcd < col_len), 1.0, 0.0).astype(F32)
        right = sigmoid(proj[:, 2 * CH : 3 * CH]) * proj[:, 3 * CH : 4 * CH] * live
        scratch_ref[...] = right
        for k in range(kcd):
            right_ref[k] = scratch_ref[pl.ds(k, rows, stride=kcd), :].astype(BF16)
        left = sigmoid(proj[:, :CH]) * proj[:, CH : 2 * CH] * live
        left_ref[...] = left.astype(BF16).reshape(rows, kcd, width)

    return kernel


def gate_kernel(pair_ref, gains_ref, w_ref, out_ref):
    rows, cols, width = pair_ref.shape
    step = 2

    def body(t, carry):
        at = pl.ds(t * step, step)
        x = pair_ref[at].reshape(step * cols, width).astype(F32)
        normed = layer_norm(x, gains_ref[2:3, :]).astype(BF16)
        out_ref[at] = sigmoid(dot(normed, w_ref[:, 4 * CH :])).reshape(step, cols, width)
        return carry

    lax.fori_loop(0, rows // step, body, 0, unroll=unroll_of(rows // step, cols))


def add_sums(left_ref, lefts, rights, sum_ref, places):
    rows = sum_ref.shape[0]
    kcd, width = lefts[0].shape[1:]
    blk = rights[0].shape[2]
    group = 8
    for d, left in enumerate(lefts):
        left_ref[d] = left[...].reshape(rows * kcd, width).astype(F32)
    for right_ref, place in zip(rights, places):
        first = pl.multiple_of(place * blk, blk)

        def sums(g, carry, right_ref=right_ref, first=first):
            acc = [jnp.zeros((blk, width), F32) for _ in range(group)]
            for d in range(len(lefts)):
                for k in range(kcd):
                    right = right_ref[d, k].astype(F32)
                    for u in range(group):
                        left = left_ref[d, pl.ds((g * group + u) * kcd + k, 1), :]
                        acc[u] = acc[u] + left * right
            for u in range(group):
                sum_ref[g * group + u, pl.ds(first, blk), :] = acc[u]
            return carry

        lax.fori_loop(0, rows // group, sums, 0)


def make_sum_kernel(n_col, blocks, place):
    def kernel(*refs):
        lefts = refs[:n_col]
        rights = refs[n_col : n_col + len(blocks)]
        sum_ref, left_ref = refs[-2:]
        add_sums(left_ref, lefts, rights, sum_ref, [place(s) for s in blocks])

    return kernel


def make_tri_kernel(n_col, blocks, place):
    def kernel(*refs):
        lefts = refs[:n_col]
        rights = refs[n_col : n_col + len(blocks)]
        pair_ref, gate_ref, gains_ref, w_ref, bias_w_ref = refs[
            n_col + len(blocks) : n_col + len(blocks) + 5
        ]
        mid_ref, norm_ref, bias_ref, sum_ref, left_ref, bias_scr = refs[-6:]
        rows, cols, width = pair_ref.shape
        add_sums(left_ref, lefts, rights, sum_ref, [place(s) for s in blocks])
        step = 2

        def finish(t, carry):
            at = pl.ds(t * step, step)
            total = sum_ref[at].reshape(step * cols, width)
            normed = layer_norm(total, gains_ref[0:1, :]).astype(BF16)
            update = dot(normed, w_ref[...])
            pair = pair_ref[at].reshape(step * cols, width).astype(F32)
            gate = gate_ref[at].reshape(step * cols, width)
            mid = (pair + gate * update).astype(BF16)
            mid_ref[at] = mid.reshape(step, cols, width)
            att = layer_norm(mid.astype(F32), gains_ref[1:2, :]).astype(BF16)
            norm_ref[at] = att.reshape(step, cols, width)
            bias = dot_nt(bias_w_ref[...], att)
            for u in range(step):
                bias_scr[t * step + u] = bias[:, u * cols : (u + 1) * cols]
            return carry

        lax.fori_loop(0, rows // step, finish, 0, unroll=unroll_of(rows // step, cols))
        for h in range(H):
            bias_ref[h] = bias_scr[:, h, :].astype(BF16)

    return kernel


def project_kernel(norm_ref, w_ref, q_ref, k_ref, v_ref, gate_ref):
    rows, cols, width = norm_ref.shape
    step = 2

    def body(t, carry):
        at = pl.ds(t * step, step)
        out = dot(norm_ref[at].reshape(step * cols, width), w_ref[...])
        shape = (step, cols, width)
        q_ref[at] = out[:, :width].astype(BF16).reshape(shape)
        k_ref[at] = out[:, width : 2 * width].astype(BF16).reshape(shape)
        v_ref[at] = out[:, 2 * width : 3 * width].astype(BF16).reshape(shape)
        gate_ref[at] = sigmoid(out[:, 3 * width :]).reshape(shape)
        return carry

    lax.fori_loop(0, rows // step, body, 0, unroll=unroll_of(rows // step, cols))


def make_spread_kernel(n_col):
    def kernel(*refs):
        others = refs[: n_col - 1]
        k_ref, v_ref, gains_ref, kv_w_ref, keys_ref, values_ref = refs[n_col - 1 :]
        rows, cols, width = k_ref.shape
        step = 2

        def spread(t, carry):
            at = pl.ds(t * step, step)
            keys_ref[at, 0:cols] = k_ref[at]
            values_ref[at, 0:cols] = v_ref[at]
            for d in range(n_col - 1):
                there = others[d][at].reshape(step * cols, width).astype(F32)
                normed = layer_norm(there, gains_ref[1:2, :]).astype(BF16)
                kv = dot(normed, kv_w_ref[:, width : 3 * width]).astype(BF16)
                low = (d + 1) * cols
                keys_ref[at, low : low + cols] = kv[:, :width].reshape(step, cols, width)
                values_ref[at, low : low + cols] = kv[:, width:].reshape(step, cols, width)
            return carry

        lax.fori_loop(0, rows // step, spread, 0, unroll=unroll_of(rows // step, cols))

    return kernel


def make_attend_kernel(n_col, n_blk, place):
    def kernel(*refs):
        biases = refs[:n_blk]
        q_ref, keys_ref, values_ref, gate_ref, mid_ref, live_ref, out_w_ref = refs[
            n_blk : n_blk + 7
        ]
        out_ref, bias_ref = refs[n_blk + 7 :]
        rows, cols, width = q_ref.shape
        blk = biases[0].shape[2]
        for d in range(n_col):
            live = jnp.broadcast_to(live_ref[:, d * cols : (d + 1) * cols], (blk, cols)) > 0.5
            for s in range(n_blk):
                first = place(s) * blk
                for h in range(H):
                    at = pl.multiple_of(h * cols + first, blk)
                    value = biases[s][d, h].astype(F32)
                    bias_ref[pl.ds(at, blk), d * cols : (d + 1) * cols] = jnp.where(
                        live, value, NEG_SCORE
                    )
        head = lax.broadcasted_iota(jnp.int32, (cols, width), 1) // DH
        scale = 1.0 / math.sqrt(DH)
        ones = jnp.ones((n_col * cols, width), BF16)

        step = 2

        def attend(i, carry):
            key = keys_ref[i]
            value = jnp.concatenate([values_ref[i], ones], axis=1)
            query = q_ref[i]
            stack = jnp.concatenate(
                [jnp.where(head == h, query, jnp.zeros_like(query)) for h in range(H)], axis=0
            )
            scores = dot_nt(stack, key) * scale + bias_ref[...]
            top = jnp.max(scores, axis=-1, keepdims=True)
            weights = jnp.exp(scores - top).astype(BF16)
            both = dot(weights, value)
            summed = both[:cols, :width]
            totals = both[:cols, width:]
            for h in range(1, H):
                mine = head == h
                part = both[h * cols : (h + 1) * cols]
                summed = jnp.where(mine, part[:, :width], summed)
                totals = jnp.where(mine, part[:, width:], totals)
            out_ref[i] = (summed / totals * gate_ref[i]).astype(BF16)
            return carry

        lax.fori_loop(0, rows, attend, 0, unroll=max(1, min(rows, 2**18 // (cols * n_col * cols))))

        def finish(t, carry):
            at = pl.ds(t * step, step)
            attended = out_ref[at].reshape(step * cols, width)
            new = mid_ref[at].reshape(step * cols, width).astype(F32) + dot(attended, out_w_ref[...])
            out_ref[at] = new.astype(BF16).reshape(step, cols, width)
            return carry

        lax.fori_loop(0, rows // step, finish, 0, unroll=unroll_of(rows // step, cols))

    return kernel


class Grid:
    def __init__(self, n_row, n_col):
        self.n_row = n_row
        self.n_col = n_col
        self.n_blk = n_row // n_col
        self.fast = n_col == 2 and n_row & (n_row - 1) == 0
        self.offsets = [0]
        if self.fast:
            bit = self.n_blk // 2
            while bit:
                self.offsets = self.offsets + [o ^ bit for o in self.offsets]
                bit //= 2

    def groups(self):
        if not self.fast or self.n_blk < 8:
            return [], list(range(self.n_blk))
        half = self.n_blk // 2
        parts = [range(half // 2), range(half // 2, half - 1), range(half - 1, half)]
        groups = [[t for s in part for t in (s, s + half)] for part in parts]
        return groups[:-1] + [groups[-1][:1]], groups[-1][1:]

    def place(self, s):
        if self.fast:
            return (lax.axis_index("row") & (self.n_blk - 1)) ^ self.offsets[s]
        return s

    def col_of(self, d):
        return (lax.axis_index("col") + d) % self.n_col

    def move(self, value, target):
        pairs = []
        for r in range(self.n_row):
            for c in range(self.n_col):
                to = target(r, c)
                if to is not None:
                    pairs.append((r * self.n_col + c, to[0] * self.n_col + to[1]))
        return lax.ppermute(value, ("row", "col"), pairs)

    def shift_col(self, value, d):
        return self.move(value, lambda r, c: (r, (c - d) % self.n_col))

    def flip_row(self, value, bit):
        return self.move(value, lambda r, c: (r ^ bit, c))

    def gather(self, own, relay):
        if not self.fast:
            stacked = lax.all_gather(own, "row", axis=0)
            stacked = lax.all_to_all(stacked, "col", split_axis=0, concat_axis=0, tiled=True)
            stacked = stacked.reshape((self.n_col, self.n_blk) + own.shape)
            order = (lax.axis_index("col") + jnp.arange(self.n_col)) % self.n_col
            stacked = jnp.take(stacked, order, axis=0)
            return [stacked[:, s] for s in range(self.n_blk)]
        half = self.n_row // 2
        same = lax.axis_index("row") // half == lax.axis_index("col")

        def inside(r, c):
            return r // half == c

        if relay:
            near = self.move(own, lambda r, c: None if inside(r, c) else (r, 1 - c))
            both = jnp.stack([own, near])
            far = self.move(both, lambda r, c: (r ^ half, c) if inside(r, c) else None)
            pair = jnp.where(same, both, far)
        else:

            def first(r, c):
                return (r ^ half, c) if inside(r, c) else (r, 1 - c)

            def second(r, c):
                return None if inside(r, c) else (r ^ half, 1 - c)

            near = self.move(own, first)
            far = self.move(own, second)
            pair = jnp.where(same, jnp.stack([own, near]), jnp.stack([near, far]))
        blocks = [pair]
        bit = self.n_blk // 2
        while bit:
            moved = []
            for at, block in enumerate(blocks):
                far_bits = bit ^ self.offsets[at]
                if relay and bit > 1:
                    moved.append(self.flip_row(pair, far_bits))
                else:
                    moved.append(self.flip_row(block, bit))
            blocks = blocks + moved
            bit //= 2
        return blocks


def make_body(grid):
    def body(
        pair_rep, chain_len, tri_gain, tri_in, sum_gain, tri_out, att_gain, att_in, att_bias, att_out
    ):
        rows, cols, width = pair_rep.shape
        n_col, n_blk = grid.n_col, grid.n_blk
        whole = (rows, cols, width)
        limit = min(60 * MIB, 12 * MIB + 24 * H * cols * n_col * cols * 4)
        tri_gain = tri_gain.reshape(1, width)
        sum_gain = sum_gain.reshape(1, width)
        att_gain = att_gain.reshape(1, width)

        anywhere = pl.BlockSpec(memory_space=pl.ANY)
        small = pl.BlockSpec(memory_space=pltpu.VMEM)
        held = limit < RESIDENT_LIMIT
        shape = pltpu.VMEM if held else jax.ShapeDtypeStruct
        left, right, gains, live = pl.pallas_call(
            make_edge_kernel(cols, n_col, grid.col_of),
            name="edges",
            out_shape=(
                shape((rows, KCD, width), BF16),
                shape((KCD, rows, width), BF16),
                shape((3, width), F32),
                shape((1, n_col * cols), F32),
            ),
            in_specs=[
                pl.BlockSpec(memory_space=pltpu.SMEM),
                anywhere,
                small,
                small,
                small,
                anywhere,
            ],
            out_specs=(small, small, small, small),
            scratch_shapes=[
                pltpu.VMEM((rows * KCD, width), F32),
                pltpu.VMEM((rows, KCD, width), BF16),
                pltpu.VMEM((width, 4 * CH), BF16),
                pltpu.SemaphoreType.DMA((2,)),
            ],
        )(chain_len, pair_rep, tri_gain, sum_gain, att_gain, tri_in)
        rights = grid.gather(right, False)
        lefts = [left] + [grid.shift_col(left, d) for d in range(1, n_col)]
        gate = call(gate_kernel, jax.ShapeDtypeStruct(whole, F32), 0, 3, limit)(
            pair_rep, gains, tri_in
        )
        early, last = grid.groups()
        left_scr = pltpu.VMEM((n_col, rows * KCD, width), F32)
        sums = []
        for blocks in early:
            sums = [
                call(
                    make_sum_kernel(n_col, blocks, grid.place),
                    jax.ShapeDtypeStruct(whole, F32),
                    0,
                    n_col + len(blocks) + len(sums),
                    limit,
                    [left_scr],
                    aliases={n_col + len(blocks): 0} if sums else {},
                )(*lefts, *[rights[s] for s in blocks], *sums)
            ]
        mid, normed, bias, _ = call(
            make_tri_kernel(n_col, last, grid.place),
            (
                jax.ShapeDtypeStruct(whole, BF16),
                jax.ShapeDtypeStruct(whole, BF16),
                jax.ShapeDtypeStruct((H, rows, cols), BF16),
                jax.ShapeDtypeStruct(whole, F32),
            ),
            0,
            n_col + len(last) + 5 + len(sums),
            limit,
            [left_scr, pltpu.VMEM((rows, H, cols), F32)],
            aliases={n_col + len(last) + 5: 3} if sums else {},
        )(*lefts, *[rights[s] for s in last], pair_rep, gate, gains, tri_out, att_bias.T, *sums)
        biases = grid.gather(bias, True)
        others = [grid.shift_col(mid, d) for d in range(1, n_col)]
        wide = jax.ShapeDtypeStruct(whole, BF16)
        query, key, value, att_gate = call(
            project_kernel, (wide, wide, wide, jax.ShapeDtypeStruct(whole, F32)), 0, 2, limit
        )(normed, att_in)
        all_keys = jax.ShapeDtypeStruct((rows, n_col * cols, width), BF16)
        keys, values = call(
            make_spread_kernel(n_col), (all_keys, all_keys), 0, n_col + 3, limit
        )(*others, key, value, gains, att_in)
        return call(
            make_attend_kernel(n_col, n_blk, grid.place),
            wide,
            0,
            n_blk + 7,
            limit,
            [pltpu.VMEM((H * cols, n_col * cols), F32)],
            held_out=False,
        )(*biases, query, keys, values, att_gate, mid, live, att_out)

    return body


def solution(mesh):
    grid = Grid(mesh.shape["row"], mesh.shape["col"])
    placed = (P("row", "col", None), P(), P(), P(), P(), P(), P(), P(), P(), P())
    return jax.shard_map(
        make_body(grid), mesh=mesh, in_specs=placed, out_specs=P("row", "col", None), check_vma=False
    )
```

```python
import math

import jax
import jax.numpy as jnp
from jax import lax
from jax.experimental import pallas as pl
from jax.experimental.pallas import tpu as pltpu
from jax.sharding import PartitionSpec as P


CH = 128
H = 4
DH = 32
KCD = 16
SLOT = 64

EPSILON = 1e-05
NEG_SCORE = -1e30
MIB = 1024 * 1024
RESIDENT_LIMIT = 32 * MIB

F32 = jnp.float32
BF16 = jnp.bfloat16


def layer_norm(values, norm_gain):
    centre = values - jnp.mean(values, axis=-1, keepdims=True)
    spread = jnp.mean(centre * centre, axis=-1, keepdims=True)
    return centre * lax.rsqrt(spread + EPSILON) * norm_gain


def sigmoid(values):
    return jax.nn.sigmoid(values)


def unroll_of(count, cols):
    return max(1, min(count, 1024 // cols))


def dot(a, b):
    return jnp.dot(a, b, preferred_element_type=F32)


def dot_nt(a, b):
    return lax.dot_general(a, b, (((1,), (1,)), ((), ())), preferred_element_type=F32)


def call(kernel, out_shape, n_smem, n_in, limit, scratch=(), held_out=True, aliases=None):
    smem = pl.BlockSpec(memory_space=pltpu.SMEM)
    vmem = pl.BlockSpec(memory_space=pltpu.VMEM)
    outs = jax.tree.map(lambda _: vmem, out_shape)
    resident = limit < RESIDENT_LIMIT
    if resident and held_out:
        out_shape = jax.tree.map(lambda o: pltpu.VMEM(o.shape, o.dtype), out_shape)
    run = pl.pallas_call(
        kernel,
        out_shape=out_shape,
        in_specs=[smem] * n_smem + [vmem] * n_in,
        out_specs=outs,
        scratch_shapes=list(scratch),
        input_output_aliases=aliases or {},
        compiler_params=pltpu.CompilerParams(vmem_limit_bytes=limit),
    )

    def apply(*args):
        if not resident:
            return run(*args)
        held = [pltpu.with_memory_space_constraint(a, pltpu.VMEM) for a in args[n_smem:]]
        return run(*args[:n_smem], *held)

    return apply


def make_edge_kernel(cols, n_col, col_of):
    def kernel(len_ref, pair_ref, gain_ref, sum_gain_ref, att_gain_ref, w_ref, *rest):
        left_ref, right_ref, gains_ref, live_ref, scratch_ref, group_ref, proj_ref, sems = rest
        rows, kcd, width = group_ref.shape
        group_copy = pltpu.make_async_copy(pair_ref.at[:, 0:kcd, :], group_ref, sems.at[0])
        proj_copy = pltpu.make_async_copy(w_ref.at[:, 0 : 4 * CH], proj_ref, sems.at[1])
        group_copy.start()
        proj_copy.start()
        row_start = lax.axis_index("row") * rows
        col_start = lax.axis_index("col") * cols
        cells = rows * kcd
        gains_ref[0:1, :] = sum_gain_ref[...]
        gains_ref[1:2, :] = att_gain_ref[...]
        gains_ref[2:3, :] = gain_ref[...]
        chains = cols // SLOT
        lane = lax.broadcasted_iota(jnp.int32, (1, cols), 1)
        for d in range(n_col):
            limit = jnp.zeros((1, cols), jnp.int32)
            for q in range(chains):
                length = len_ref[col_of(d) * chains + q]
                limit = jnp.where(lane // SLOT == q, q * SLOT + length, limit)
            live_ref[:, d * cols : (d + 1) * cols] = jnp.where(lane < limit, 1.0, 0.0).astype(F32)
        group_copy.wait()
        normed = layer_norm(group_ref[...].reshape(cells, width).astype(F32), gain_ref[...])
        proj_copy.wait()
        proj = dot(normed.astype(BF16), proj_ref[...])
        row_len = len_ref[row_start // SLOT]
        row_base = row_start % SLOT
        col_len = len_ref[col_start // SLOT]
        cell = lax.broadcasted_iota(jnp.int32, (cells, width), 0)
        row_live = (cell // kcd + row_base) < row_len
        live = jnp.where(row_live & (cell % kcd < col_len), 1.0, 0.0).astype(F32)
        right = sigmoid(proj[:, 2 * CH : 3 * CH]) * proj[:, 3 * CH : 4 * CH] * live
        scratch_ref[...] = right
        for k in range(kcd):
            right_ref[k] = scratch_ref[pl.ds(k, rows, stride=kcd), :].astype(BF16)
        left = sigmoid(proj[:, :CH]) * proj[:, CH : 2 * CH] * live
        left_ref[...] = left.astype(BF16).reshape(rows, kcd, width)

    return kernel


def gate_kernel(pair_ref, gains_ref, w_ref, out_ref):
    rows, cols, width = pair_ref.shape
    step = 2

    def body(t, carry):
        at = pl.ds(t * step, step)
        x = pair_ref[at].reshape(step * cols, width).astype(F32)
        normed = layer_norm(x, gains_ref[2:3, :]).astype(BF16)
        out_ref[at] = sigmoid(dot(normed, w_ref[:, 4 * CH :])).reshape(step, cols, width)
        return carry

    lax.fori_loop(0, rows // step, body, 0, unroll=unroll_of(rows // step, cols))


def add_sums(left_ref, lefts, rights, sum_ref, places):
    rows = sum_ref.shape[0]
    kcd, width = lefts[0].shape[1:]
    blk = rights[0].shape[2]
    group = 8
    for d, left in enumerate(lefts):
        left_ref[d] = left[...].reshape(rows * kcd, width).astype(F32)
    for right_ref, place in zip(rights, places):
        first = pl.multiple_of(place * blk, blk)

        def sums(g, carry, right_ref=right_ref, first=first):
            acc = [jnp.zeros((blk, width), F32) for _ in range(group)]
            for d in range(len(lefts)):
                for k in range(kcd):
                    right = right_ref[d, k].astype(F32)
                    for u in range(group):
                        left = left_ref[d, pl.ds((g * group + u) * kcd + k, 1), :]
                        acc[u] = acc[u] + left * right
            for u in range(group):
                sum_ref[g * group + u, pl.ds(first, blk), :] = acc[u]
            return carry

        lax.fori_loop(0, rows // group, sums, 0)


def make_sum_kernel(n_col, blocks, place):
    def kernel(*refs):
        lefts = refs[:n_col]
        rights = refs[n_col : n_col + len(blocks)]
        sum_ref, left_ref = refs[-2:]
        add_sums(left_ref, lefts, rights, sum_ref, [place(s) for s in blocks])

    return kernel


def make_tri_kernel(n_col, blocks, place, parts):
    def kernel(*refs):
        lefts = refs[:n_col]
        rights = refs[n_col : n_col + len(blocks)]
        pair_ref, gate_ref, gains_ref, w_ref, bias_w_ref = refs[
            n_col + len(blocks) : n_col + len(blocks) + 5
        ]
        mid_refs = refs[-5 - parts : -5]
        norm_ref, bias_ref, sum_ref, left_ref, bias_scr = refs[-5:]
        rows, cols, width = pair_ref.shape
        add_sums(left_ref, lefts, rights, sum_ref, [place(s) for s in blocks])
        step = 2

        share = rows // parts // step
        for part, mid_ref in enumerate(mid_refs):

            def finish(t, carry, part=part, mid_ref=mid_ref):
                row = part * share * step + t * step
                at = pl.ds(row, step)
                total = sum_ref[at].reshape(step * cols, width)
                normed = layer_norm(total, gains_ref[0:1, :]).astype(BF16)
                update = dot(normed, w_ref[...])
                pair = pair_ref[at].reshape(step * cols, width).astype(F32)
                gate = gate_ref[at].reshape(step * cols, width)
                mid = (pair + gate * update).astype(BF16)
                mid_ref[pl.ds(t * step, step)] = mid.reshape(step, cols, width)
                att = layer_norm(mid.astype(F32), gains_ref[1:2, :]).astype(BF16)
                norm_ref[at] = att.reshape(step, cols, width)
                bias = dot_nt(bias_w_ref[...], att)
                for u in range(step):
                    bias_scr[row + u] = bias[:, u * cols : (u + 1) * cols]
                return carry

            lax.fori_loop(0, share, finish, 0, unroll=unroll_of(share, cols))
        for h in range(H):
            bias_ref[h] = bias_scr[:, h, :].astype(BF16)

    return kernel


def project_kernel(norm_ref, w_ref, q_ref, k_ref, v_ref, gate_ref):
    rows, cols, width = norm_ref.shape
    step = 2

    def body(t, carry):
        at = pl.ds(t * step, step)
        out = dot(norm_ref[at].reshape(step * cols, width), w_ref[...])
        shape = (step, cols, width)
        q_ref[at] = out[:, :width].astype(BF16).reshape(shape)
        k_ref[at] = out[:, width : 2 * width].astype(BF16).reshape(shape)
        v_ref[at] = out[:, 2 * width : 3 * width].astype(BF16).reshape(shape)
        gate_ref[at] = sigmoid(out[:, 3 * width :]).reshape(shape)
        return carry

    lax.fori_loop(0, rows // step, body, 0, unroll=unroll_of(rows // step, cols))


def make_spread_kernel(n_col, base):
    def kernel(*refs):
        others = refs[: n_col - 1]
        k_ref, v_ref, gains_ref, kv_w_ref, keys_ref, values_ref = refs[n_col - 1 :]
        rows = keys_ref.shape[0]
        cols, width = k_ref.shape[1:]
        step = 2

        def spread(t, carry):
            at = pl.ds(t * step, step)
            own = pl.ds(base + t * step, step)
            keys_ref[at, 0:cols] = k_ref[own]
            values_ref[at, 0:cols] = v_ref[own]
            for d in range(n_col - 1):
                there = others[d][at].reshape(step * cols, width).astype(F32)
                normed = layer_norm(there, gains_ref[1:2, :]).astype(BF16)
                kv = dot(normed, kv_w_ref[:, width : 3 * width]).astype(BF16)
                low = (d + 1) * cols
                keys_ref[at, low : low + cols] = kv[:, :width].reshape(step, cols, width)
                values_ref[at, low : low + cols] = kv[:, width:].reshape(step, cols, width)
            return carry

        lax.fori_loop(0, rows // step, spread, 0, unroll=unroll_of(rows // step, cols))

    return kernel


def make_attend_kernel(n_col, n_blk, place, base, n_done):
    def kernel(*refs):
        biases = refs[:n_blk]
        q_ref, keys_ref, values_ref, gate_ref, mid_ref, live_ref, out_w_ref = refs[
            n_blk : n_blk + 7
        ]
        done = refs[n_blk + 7 : n_blk + 7 + n_done]
        whole_ref, bias_ref = refs[n_blk + 7 + n_done :]
        rows, cols, width = mid_ref.shape
        first_row = base if n_done else 0
        out_ref = whole_ref.at[first_row : first_row + rows]
        for at, done_ref in enumerate(done):
            whole_ref[at * rows : (at + 1) * rows] = done_ref[...]
        blk = biases[0].shape[2]
        for d in range(n_col):
            live = jnp.broadcast_to(live_ref[:, d * cols : (d + 1) * cols], (blk, cols)) > 0.5
            for s in range(n_blk):
                first = place(s) * blk
                for h in range(H):
                    at = pl.multiple_of(h * cols + first, blk)
                    value = biases[s][d, h].astype(F32)
                    bias_ref[pl.ds(at, blk), d * cols : (d + 1) * cols] = jnp.where(
                        live, value, NEG_SCORE
                    )
        head = lax.broadcasted_iota(jnp.int32, (cols, width), 1) // DH
        scale = 1.0 / math.sqrt(DH)
        ones = jnp.ones((n_col * cols, width), BF16)

        step = 2

        def attend(i, carry):
            key = keys_ref[i]
            value = jnp.concatenate([values_ref[i], ones], axis=1)
            query = q_ref[base + i]
            stack = jnp.concatenate(
                [jnp.where(head == h, query, jnp.zeros_like(query)) for h in range(H)], axis=0
            )
            scores = dot_nt(stack, key) * scale + bias_ref[...]
            top = jnp.max(scores, axis=-1, keepdims=True)
            weights = jnp.exp(scores - top).astype(BF16)
            both = dot(weights, value)
            summed = both[:cols, :width]
            totals = both[:cols, width:]
            for h in range(1, H):
                mine = head == h
                part = both[h * cols : (h + 1) * cols]
                summed = jnp.where(mine, part[:, :width], summed)
                totals = jnp.where(mine, part[:, width:], totals)
            out_ref[i] = (summed / totals * gate_ref[base + i]).astype(BF16)
            return carry

        lax.fori_loop(0, rows, attend, 0, unroll=max(1, min(rows, 2**18 // (cols * n_col * cols))))

        def finish(t, carry):
            at = pl.ds(t * step, step)
            attended = out_ref[at].reshape(step * cols, width)
            new = mid_ref[at].reshape(step * cols, width).astype(F32) + dot(attended, out_w_ref[...])
            out_ref[at] = new.astype(BF16).reshape(step, cols, width)
            return carry

        lax.fori_loop(0, rows // step, finish, 0, unroll=unroll_of(rows // step, cols))

    return kernel


class Grid:
    def __init__(self, n_row, n_col):
        self.n_row = n_row
        self.n_col = n_col
        self.n_blk = n_row // n_col
        self.fast = n_col == 2 and n_row & (n_row - 1) == 0
        self.offsets = [0]
        if self.fast:
            bit = self.n_blk // 2
            while bit:
                self.offsets = self.offsets + [o ^ bit for o in self.offsets]
                bit //= 2

    def groups(self):
        if not self.fast or self.n_blk < 8:
            return [], list(range(self.n_blk))
        half = self.n_blk // 2
        parts = [range(half // 2), range(half // 2, half - 1), range(half - 1, half)]
        groups = [[t for s in part for t in (s, s + half)] for part in parts]
        return groups[:-1] + [groups[-1][:1]], groups[-1][1:]

    def place(self, s):
        if self.fast:
            return (lax.axis_index("row") & (self.n_blk - 1)) ^ self.offsets[s]
        return s

    def col_of(self, d):
        return (lax.axis_index("col") + d) % self.n_col

    def move(self, value, target):
        pairs = []
        for r in range(self.n_row):
            for c in range(self.n_col):
                to = target(r, c)
                if to is not None:
                    pairs.append((r * self.n_col + c, to[0] * self.n_col + to[1]))
        return lax.ppermute(value, ("row", "col"), pairs)

    def shift_col(self, value, d):
        return self.move(value, lambda r, c: (r, (c - d) % self.n_col))

    def flip_row(self, value, bit):
        return self.move(value, lambda r, c: (r ^ bit, c))

    def gather(self, own, relay):
        if not self.fast:
            stacked = lax.all_gather(own, "row", axis=0)
            stacked = lax.all_to_all(stacked, "col", split_axis=0, concat_axis=0, tiled=True)
            stacked = stacked.reshape((self.n_col, self.n_blk) + own.shape)
            order = (lax.axis_index("col") + jnp.arange(self.n_col)) % self.n_col
            stacked = jnp.take(stacked, order, axis=0)
            return [stacked[:, s] for s in range(self.n_blk)]
        half = self.n_row // 2
        same = lax.axis_index("row") // half == lax.axis_index("col")

        def inside(r, c):
            return r // half == c

        if relay:
            near = self.move(own, lambda r, c: None if inside(r, c) else (r, 1 - c))
            both = jnp.stack([own, near])
            far = self.move(both, lambda r, c: (r ^ half, c) if inside(r, c) else None)
            pair = jnp.where(same, both, far)
        else:

            def first(r, c):
                return (r ^ half, c) if inside(r, c) else (r, 1 - c)

            def second(r, c):
                return None if inside(r, c) else (r ^ half, 1 - c)

            near = self.move(own, first)
            far = self.move(own, second)
            pair = jnp.where(same, jnp.stack([own, near]), jnp.stack([near, far]))
        blocks = [pair]
        bit = self.n_blk // 2
        while bit:
            moved = []
            for at, block in enumerate(blocks):
                far_bits = bit ^ self.offsets[at]
                if relay and bit > 1:
                    moved.append(self.flip_row(pair, far_bits))
                else:
                    moved.append(self.flip_row(block, bit))
            blocks = blocks + moved
            bit //= 2
        return blocks


def make_body(grid):
    def body(
        pair_rep, chain_len, tri_gain, tri_in, sum_gain, tri_out, att_gain, att_in, att_bias, att_out
    ):
        rows, cols, width = pair_rep.shape
        n_col, n_blk = grid.n_col, grid.n_blk
        whole = (rows, cols, width)
        parts = 2 if grid.fast else 1
        limit = min(60 * MIB, 12 * MIB + 24 * H * cols * n_col * cols * 4)
        tri_gain = tri_gain.reshape(1, width)
        sum_gain = sum_gain.reshape(1, width)
        att_gain = att_gain.reshape(1, width)

        anywhere = pl.BlockSpec(memory_space=pl.ANY)
        small = pl.BlockSpec(memory_space=pltpu.VMEM)
        held = limit < RESIDENT_LIMIT
        shape = pltpu.VMEM if held else jax.ShapeDtypeStruct
        left, right, gains, live = pl.pallas_call(
            make_edge_kernel(cols, n_col, grid.col_of),
            name="edges",
            out_shape=(
                shape((rows, KCD, width), BF16),
                shape((KCD, rows, width), BF16),
                shape((3, width), F32),
                shape((1, n_col * cols), F32),
            ),
            in_specs=[
                pl.BlockSpec(memory_space=pltpu.SMEM),
                anywhere,
                small,
                small,
                small,
                anywhere,
            ],
            out_specs=(small, small, small, small),
            scratch_shapes=[
                pltpu.VMEM((rows * KCD, width), F32),
                pltpu.VMEM((rows, KCD, width), BF16),
                pltpu.VMEM((width, 4 * CH), BF16),
                pltpu.SemaphoreType.DMA((2,)),
            ],
        )(chain_len, pair_rep, tri_gain, sum_gain, att_gain, tri_in)
        rights = grid.gather(right, False)
        lefts = [left] + [grid.shift_col(left, d) for d in range(1, n_col)]
        gate = call(gate_kernel, jax.ShapeDtypeStruct(whole, F32), 0, 3, limit)(
            pair_rep, gains, tri_in
        )
        early, last = grid.groups()
        left_scr = pltpu.VMEM((n_col, rows * KCD, width), F32)
        sums = []
        for blocks in early:
            sums = [
                call(
                    make_sum_kernel(n_col, blocks, grid.place),
                    jax.ShapeDtypeStruct(whole, F32),
                    0,
                    n_col + len(blocks) + len(sums),
                    limit,
                    [left_scr],
                    aliases={n_col + len(blocks): 0} if sums else {},
                )(*lefts, *[rights[s] for s in blocks], *sums)
            ]
        *mids, normed, bias, _ = call(
            make_tri_kernel(n_col, last, grid.place, parts),
            (
                *[jax.ShapeDtypeStruct((rows // parts, cols, width), BF16)] * parts,
                jax.ShapeDtypeStruct(whole, BF16),
                jax.ShapeDtypeStruct((H, rows, cols), BF16),
                jax.ShapeDtypeStruct(whole, F32),
            ),
            0,
            n_col + len(last) + 5 + len(sums),
            limit,
            [left_scr, pltpu.VMEM((rows, H, cols), F32)],
            aliases={n_col + len(last) + 5: parts + 2} if sums else {},
        )(*lefts, *[rights[s] for s in last], pair_rep, gate, gains, tri_out, att_bias.T, *sums)
        biases = grid.gather(bias, True)
        others = []
        for mid in mids:
            others.append([grid.shift_col(mid, d) for d in range(1, n_col)])
        wide = jax.ShapeDtypeStruct(whole, BF16)
        query, key, value, att_gate = call(
            project_kernel, (wide, wide, wide, jax.ShapeDtypeStruct(whole, F32)), 0, 2, limit
        )(normed, att_in)
        share = rows // parts
        all_keys = jax.ShapeDtypeStruct((share, n_col * cols, width), BF16)
        done = []
        for part in range(parts):
            base = part * share
            final = part == parts - 1
            keys, values = call(
                make_spread_kernel(n_col, base), (all_keys, all_keys), 0, n_col + 3, limit
            )(*others[part], key, value, gains, att_in)
            result = call(
                make_attend_kernel(n_col, n_blk, grid.place, base, len(done) * final),
                wide if final else jax.ShapeDtypeStruct((share, cols, width), BF16),
                0,
                n_blk + 7 + len(done) * final,
                limit,
                [pltpu.VMEM((H * cols, n_col * cols), F32)],
                held_out=not final,
            )(
                *biases,
                query,
                keys,
                values,
                att_gate,
                mids[part],
                live,
                att_out,
                *(done if final else []),
            )
            done.append(result)
        return result

    return body


def solution(mesh):
    grid = Grid(mesh.shape["row"], mesh.shape["col"])
    placed = (P("row", "col", None), P(), P(), P(), P(), P(), P(), P(), P(), P())
    return jax.shard_map(
        make_body(grid), mesh=mesh, in_specs=placed, out_specs=P("row", "col", None), check_vma=False
    )
```

```python
import math

import jax
import jax.numpy as jnp
from jax import lax
from jax.experimental import pallas as pl
from jax.experimental.pallas import tpu as pltpu
from jax.sharding import PartitionSpec as P


CH = 128
H = 4
DH = 32
KCD = 16
SLOT = 64

EPSILON = 1e-05
NEG_SCORE = -1e30
MIB = 1024 * 1024
RESIDENT_LIMIT = 32 * MIB

F32 = jnp.float32
BF16 = jnp.bfloat16


def layer_norm(values, norm_gain):
    centre = values - jnp.mean(values, axis=-1, keepdims=True)
    spread = jnp.mean(centre * centre, axis=-1, keepdims=True)
    return centre * lax.rsqrt(spread + EPSILON) * norm_gain


def sigmoid(values):
    return jax.nn.sigmoid(values)


def unroll_of(count, cols):
    return max(1, min(count, 1024 // cols))


def dot(a, b):
    return jnp.dot(a, b, preferred_element_type=F32)


def dot_nt(a, b):
    return lax.dot_general(a, b, (((1,), (1,)), ((), ())), preferred_element_type=F32)


def call(kernel, out_shape, n_smem, n_in, limit, scratch=(), held_out=True, aliases=None):
    smem = pl.BlockSpec(memory_space=pltpu.SMEM)
    vmem = pl.BlockSpec(memory_space=pltpu.VMEM)
    outs = jax.tree.map(lambda _: vmem, out_shape)
    resident = limit < RESIDENT_LIMIT
    if resident and held_out:
        out_shape = jax.tree.map(lambda o: pltpu.VMEM(o.shape, o.dtype), out_shape)
    run = pl.pallas_call(
        kernel,
        out_shape=out_shape,
        in_specs=[smem] * n_smem + [vmem] * n_in,
        out_specs=outs,
        scratch_shapes=list(scratch),
        input_output_aliases=aliases or {},
        compiler_params=pltpu.CompilerParams(vmem_limit_bytes=limit),
    )

    def apply(*args):
        if not resident:
            return run(*args)
        held = [pltpu.with_memory_space_constraint(a, pltpu.VMEM) for a in args[n_smem:]]
        return run(*args[:n_smem], *held)

    return apply


def make_edge_kernel(cols, n_col, col_of):
    def kernel(len_ref, pair_ref, gain_ref, sum_gain_ref, att_gain_ref, w_ref, *rest):
        left_ref, right_ref, gains_ref, live_ref, scratch_ref, group_ref, proj_ref, sems = rest
        rows, kcd, width = group_ref.shape
        group_copy = pltpu.make_async_copy(pair_ref.at[:, 0:kcd, :], group_ref, sems.at[0])
        proj_copy = pltpu.make_async_copy(w_ref.at[:, 0 : 4 * CH], proj_ref, sems.at[1])
        group_copy.start()
        proj_copy.start()
        row_start = lax.axis_index("row") * rows
        col_start = lax.axis_index("col") * cols
        cells = rows * kcd
        gains_ref[0:1, :] = sum_gain_ref[...]
        gains_ref[1:2, :] = att_gain_ref[...]
        gains_ref[2:3, :] = gain_ref[...]
        chains = cols // SLOT
        lane = lax.broadcasted_iota(jnp.int32, (1, cols), 1)
        for d in range(n_col):
            limit = jnp.zeros((1, cols), jnp.int32)
            for q in range(chains):
                length = len_ref[col_of(d) * chains + q]
                limit = jnp.where(lane // SLOT == q, q * SLOT + length, limit)
            live_ref[:, d * cols : (d + 1) * cols] = jnp.where(lane < limit, 1.0, 0.0).astype(F32)
        group_copy.wait()
        normed = layer_norm(group_ref[...].reshape(cells, width).astype(F32), gain_ref[...])
        proj_copy.wait()
        proj = dot(normed.astype(BF16), proj_ref[...])
        row_len = len_ref[row_start // SLOT]
        row_base = row_start % SLOT
        col_len = len_ref[col_start // SLOT]
        cell = lax.broadcasted_iota(jnp.int32, (cells, width), 0)
        row_live = (cell // kcd + row_base) < row_len
        live = jnp.where(row_live & (cell % kcd < col_len), 1.0, 0.0).astype(F32)
        right = sigmoid(proj[:, 2 * CH : 3 * CH]) * proj[:, 3 * CH : 4 * CH] * live
        scratch_ref[...] = right
        for k in range(kcd):
            right_ref[k] = scratch_ref[pl.ds(k, rows, stride=kcd), :].astype(BF16)
        left = sigmoid(proj[:, :CH]) * proj[:, CH : 2 * CH] * live
        left_ref[...] = left.astype(BF16).reshape(rows, kcd, width)

    return kernel


def gate_kernel(pair_ref, gains_ref, w_ref, out_ref):
    rows, cols, width = pair_ref.shape
    step = 2

    def body(t, carry):
        at = pl.ds(t * step, step)
        x = pair_ref[at].reshape(step * cols, width).astype(F32)
        normed = layer_norm(x, gains_ref[2:3, :]).astype(BF16)
        out_ref[at] = sigmoid(dot(normed, w_ref[:, 4 * CH :])).reshape(step, cols, width)
        return carry

    lax.fori_loop(0, rows // step, body, 0, unroll=unroll_of(rows // step, cols))


def add_sums(left_ref, lefts, rights, sum_ref, places):
    rows = sum_ref.shape[0]
    kcd, width = lefts[0].shape[1:]
    blk = rights[0].shape[2]
    group = 8
    for d, left in enumerate(lefts):
        left_ref[d] = left[...].reshape(rows * kcd, width).astype(F32)
    for right_ref, place in zip(rights, places):
        first = pl.multiple_of(place * blk, blk)

        def sums(g, carry, right_ref=right_ref, first=first):
            acc = [jnp.zeros((blk, width), F32) for _ in range(group)]
            for d in range(len(lefts)):
                for k in range(kcd):
                    right = right_ref[d, k].astype(F32)
                    for u in range(group):
                        left = left_ref[d, pl.ds((g * group + u) * kcd + k, 1), :]
                        acc[u] = acc[u] + left * right
            for u in range(group):
                sum_ref[g * group + u, pl.ds(first, blk), :] = acc[u]
            return carry

        lax.fori_loop(0, rows // group, sums, 0)


def make_sum_kernel(n_col, blocks, place):
    def kernel(*refs):
        lefts = refs[:n_col]
        rights = refs[n_col : n_col + len(blocks)]
        sum_ref, left_ref = refs[-2:]
        add_sums(left_ref, lefts, rights, sum_ref, [place(s) for s in blocks])

    return kernel


def make_tri_kernel(n_col, blocks, place, parts):
    def kernel(*refs):
        lefts = refs[:n_col]
        rights = refs[n_col : n_col + len(blocks)]
        pair_ref, gate_ref, gains_ref, w_ref, bias_w_ref = refs[
            n_col + len(blocks) : n_col + len(blocks) + 5
        ]
        mid_refs = refs[-5 - parts : -5]
        norm_ref, bias_ref, sum_ref, left_ref, bias_scr = refs[-5:]
        rows, cols, width = pair_ref.shape
        add_sums(left_ref, lefts, rights, sum_ref, [place(s) for s in blocks])
        step = 2

        share = rows // parts // step
        for part, mid_ref in enumerate(mid_refs):

            def finish(t, carry, part=part, mid_ref=mid_ref):
                row = part * share * step + t * step
                at = pl.ds(row, step)
                total = sum_ref[at].reshape(step * cols, width)
                normed = layer_norm(total, gains_ref[0:1, :]).astype(BF16)
                update = dot(normed, w_ref[...])
                pair = pair_ref[at].reshape(step * cols, width).astype(F32)
                gate = gate_ref[at].reshape(step * cols, width)
                mid = (pair + gate * update).astype(BF16)
                mid_ref[pl.ds(t * step, step)] = mid.reshape(step, cols, width)
                att = layer_norm(mid.astype(F32), gains_ref[1:2, :]).astype(BF16)
                norm_ref[at] = att.reshape(step, cols, width)
                bias = dot_nt(bias_w_ref[...], att)
                for u in range(step):
                    bias_scr[row + u] = bias[:, u * cols : (u + 1) * cols]
                return carry

            lax.fori_loop(0, share, finish, 0, unroll=unroll_of(share, cols))
        for h in range(H):
            bias_ref[h] = bias_scr[:, h, :].astype(BF16)

    return kernel


def project_kernel(norm_ref, w_ref, q_ref, k_ref, v_ref, gate_ref):
    rows, cols, width = norm_ref.shape
    step = 2

    def body(t, carry):
        at = pl.ds(t * step, step)
        out = dot(norm_ref[at].reshape(step * cols, width), w_ref[...])
        shape = (step, cols, width)
        q_ref[at] = out[:, :width].astype(BF16).reshape(shape)
        k_ref[at] = out[:, width : 2 * width].astype(BF16).reshape(shape)
        v_ref[at] = out[:, 2 * width : 3 * width].astype(BF16).reshape(shape)
        gate_ref[at] = sigmoid(out[:, 3 * width :]).reshape(shape)
        return carry

    lax.fori_loop(0, rows // step, body, 0, unroll=unroll_of(rows // step, cols))


def make_spread_kernel(n_col, base):
    def kernel(*refs):
        others = refs[: n_col - 1]
        k_ref, v_ref, gains_ref, kv_w_ref, keys_ref, values_ref = refs[n_col - 1 :]
        rows = keys_ref.shape[0]
        cols, width = k_ref.shape[1:]
        step = 2

        def spread(t, carry):
            at = pl.ds(t * step, step)
            own = pl.ds(base + t * step, step)
            keys_ref[at, 0:cols] = k_ref[own]
            values_ref[at, 0:cols] = v_ref[own]
            for d in range(n_col - 1):
                there = others[d][at].reshape(step * cols, width).astype(F32)
                normed = layer_norm(there, gains_ref[1:2, :]).astype(BF16)
                kv = dot(normed, kv_w_ref[:, width : 3 * width]).astype(BF16)
                low = (d + 1) * cols
                keys_ref[at, low : low + cols] = kv[:, :width].reshape(step, cols, width)
                values_ref[at, low : low + cols] = kv[:, width:].reshape(step, cols, width)
            return carry

        lax.fori_loop(0, rows // step, spread, 0, unroll=unroll_of(rows // step, cols))

    return kernel


def make_attend_kernel(n_col, n_blk, place, base, n_done):
    def kernel(*refs):
        biases = refs[:n_blk]
        q_ref, keys_ref, values_ref, gate_ref, mid_ref, live_ref, out_w_ref = refs[
            n_blk : n_blk + 7
        ]
        done = refs[n_blk + 7 : n_blk + 7 + n_done]
        whole_ref, bias_ref = refs[n_blk + 7 + n_done :]
        rows, cols, width = mid_ref.shape
        first_row = base if n_done else 0
        out_ref = whole_ref.at[first_row : first_row + rows]
        for at, done_ref in enumerate(done):
            whole_ref[at * rows : (at + 1) * rows] = done_ref[...]
        blk = biases[0].shape[2]
        for d in range(n_col):
            live = jnp.broadcast_to(live_ref[:, d * cols : (d + 1) * cols], (blk, cols)) > 0.5
            for s in range(n_blk):
                first = place(s) * blk
                for h in range(H):
                    at = pl.multiple_of(h * cols + first, blk)
                    value = biases[s][d, h].astype(F32)
                    bias_ref[pl.ds(at, blk), d * cols : (d + 1) * cols] = jnp.where(
                        live, value, NEG_SCORE
                    )
        head = lax.broadcasted_iota(jnp.int32, (cols, width), 1) // DH
        scale = 1.0 / math.sqrt(DH)
        ones = jnp.ones((n_col * cols, width), BF16)

        step = 2

        def attend(i, carry):
            key = keys_ref[i]
            value = jnp.concatenate([values_ref[i], ones], axis=1)
            query = q_ref[base + i]
            stack = jnp.concatenate(
                [jnp.where(head == h, query, jnp.zeros_like(query)) for h in range(H)], axis=0
            )
            scores = dot_nt(stack, key) * scale + bias_ref[...]
            top = jnp.max(scores, axis=-1, keepdims=True)
            weights = jnp.exp(scores - top).astype(BF16)
            both = dot(weights, value)
            summed = both[:cols, :width]
            totals = both[:cols, width:]
            for h in range(1, H):
                mine = head == h
                part = both[h * cols : (h + 1) * cols]
                summed = jnp.where(mine, part[:, :width], summed)
                totals = jnp.where(mine, part[:, width:], totals)
            out_ref[i] = (summed / totals * gate_ref[base + i]).astype(BF16)
            return carry

        lax.fori_loop(0, rows, attend, 0, unroll=max(1, min(rows, 2**18 // (cols * n_col * cols))))

        def finish(t, carry):
            at = pl.ds(t * step, step)
            attended = out_ref[at].reshape(step * cols, width)
            new = mid_ref[at].reshape(step * cols, width).astype(F32) + dot(attended, out_w_ref[...])
            out_ref[at] = new.astype(BF16).reshape(step, cols, width)
            return carry

        lax.fori_loop(0, rows // step, finish, 0, unroll=unroll_of(rows // step, cols))

    return kernel


class Grid:
    def __init__(self, n_row, n_col):
        self.n_row = n_row
        self.n_col = n_col
        self.n_blk = n_row // n_col
        self.fast = n_col == 2 and n_row & (n_row - 1) == 0
        self.offsets = [0]
        if self.fast:
            bit = self.n_blk // 2
            while bit:
                self.offsets = self.offsets + [o ^ bit for o in self.offsets]
                bit //= 2

    def groups(self):
        if not self.fast or self.n_blk < 8:
            return [], list(range(self.n_blk))
        half = self.n_blk // 2
        parts = [range(half // 2), range(half // 2 + 1, half), range(half // 2, half // 2 + 1)]
        groups = [[t for s in part for t in (s, s + half)] for part in parts]
        return groups[:-1] + [groups[-1][:1]], groups[-1][1:]

    def place(self, s):
        if self.fast:
            return (lax.axis_index("row") & (self.n_blk - 1)) ^ self.offsets[s]
        return s

    def col_of(self, d):
        return (lax.axis_index("col") + d) % self.n_col

    def move(self, value, target):
        pairs = []
        for r in range(self.n_row):
            for c in range(self.n_col):
                to = target(r, c)
                if to is not None:
                    pairs.append((r * self.n_col + c, to[0] * self.n_col + to[1]))
        return lax.ppermute(value, ("row", "col"), pairs)

    def shift_col(self, value, d):
        return self.move(value, lambda r, c: (r, (c - d) % self.n_col))

    def flip_row(self, value, bit):
        return self.move(value, lambda r, c: (r ^ bit, c))

    def gather(self, own):
        if not self.fast:
            stacked = lax.all_gather(own, "row", axis=0)
            stacked = lax.all_to_all(stacked, "col", split_axis=0, concat_axis=0, tiled=True)
            stacked = stacked.reshape((self.n_col, self.n_blk) + own.shape)
            order = (lax.axis_index("col") + jnp.arange(self.n_col)) % self.n_col
            stacked = jnp.take(stacked, order, axis=0)
            return [stacked[:, s] for s in range(self.n_blk)]
        half = self.n_row // 2
        same = lax.axis_index("row") // half == lax.axis_index("col")

        def inside(r, c):
            return r // half == c

        def first(r, c):
            return (r ^ half, c) if inside(r, c) else (r, 1 - c)

        def second(r, c):
            return None if inside(r, c) else (r ^ half, 1 - c)

        near = self.move(own, first)
        far = self.move(own, second)
        pair = jnp.where(same, jnp.stack([own, near]), jnp.stack([near, far]))
        blocks = [pair]
        bit = self.n_blk // 2
        while bit:
            moved = []
            for at, block in enumerate(blocks):
                far_bits = bit ^ self.offsets[at]
                if bit > 1:
                    moved.append(self.flip_row(pair, far_bits))
                else:
                    moved.append(self.flip_row(block, bit))
            blocks = blocks + moved
            bit //= 2
        return blocks


def make_body(grid):
    def body(
        pair_rep, chain_len, tri_gain, tri_in, sum_gain, tri_out, att_gain, att_in, att_bias, att_out
    ):
        rows, cols, width = pair_rep.shape
        n_col, n_blk = grid.n_col, grid.n_blk
        whole = (rows, cols, width)
        parts = 2 if grid.fast else 1
        limit = min(60 * MIB, 12 * MIB + 24 * H * cols * n_col * cols * 4)
        tri_gain = tri_gain.reshape(1, width)
        sum_gain = sum_gain.reshape(1, width)
        att_gain = att_gain.reshape(1, width)

        anywhere = pl.BlockSpec(memory_space=pl.ANY)
        small = pl.BlockSpec(memory_space=pltpu.VMEM)
        held = limit < RESIDENT_LIMIT
        shape = pltpu.VMEM if held else jax.ShapeDtypeStruct
        left, right, gains, live = pl.pallas_call(
            make_edge_kernel(cols, n_col, grid.col_of),
            name="edges",
            out_shape=(
                shape((rows, KCD, width), BF16),
                shape((KCD, rows, width), BF16),
                shape((3, width), F32),
                shape((1, n_col * cols), F32),
            ),
            in_specs=[
                pl.BlockSpec(memory_space=pltpu.SMEM),
                anywhere,
                small,
                small,
                small,
                anywhere,
            ],
            out_specs=(small, small, small, small),
            scratch_shapes=[
                pltpu.VMEM((rows * KCD, width), F32),
                pltpu.VMEM((rows, KCD, width), BF16),
                pltpu.VMEM((width, 4 * CH), BF16),
                pltpu.SemaphoreType.DMA((2,)),
            ],
        )(chain_len, pair_rep, tri_gain, sum_gain, att_gain, tri_in)
        rights = grid.gather(right)
        lefts = [left] + [grid.shift_col(left, d) for d in range(1, n_col)]
        gate = call(gate_kernel, jax.ShapeDtypeStruct(whole, F32), 0, 3, limit)(
            pair_rep, gains, tri_in
        )
        early, last = grid.groups()
        left_scr = pltpu.VMEM((n_col, rows * KCD, width), F32)
        sums = []
        for blocks in early:
            sums = [
                call(
                    make_sum_kernel(n_col, blocks, grid.place),
                    jax.ShapeDtypeStruct(whole, F32),
                    0,
                    n_col + len(blocks) + len(sums),
                    limit,
                    [left_scr],
                    aliases={n_col + len(blocks): 0} if sums else {},
                )(*lefts, *[rights[s] for s in blocks], *sums)
            ]
        *mids, normed, bias, _ = call(
            make_tri_kernel(n_col, last, grid.place, parts),
            (
                *[jax.ShapeDtypeStruct((rows // parts, cols, width), BF16)] * parts,
                jax.ShapeDtypeStruct(whole, BF16),
                jax.ShapeDtypeStruct((H, rows, cols), BF16),
                jax.ShapeDtypeStruct(whole, F32),
            ),
            0,
            n_col + len(last) + 5 + len(sums),
            limit,
            [left_scr, pltpu.VMEM((rows, H, cols), F32)],
            aliases={n_col + len(last) + 5: parts + 2} if sums else {},
        )(*lefts, *[rights[s] for s in last], pair_rep, gate, gains, tri_out, att_bias.T, *sums)
        biases = grid.gather(bias)
        others = []
        for mid in mids:
            others.append([grid.shift_col(mid, d) for d in range(1, n_col)])
        wide = jax.ShapeDtypeStruct(whole, BF16)
        query, key, value, att_gate = call(
            project_kernel, (wide, wide, wide, jax.ShapeDtypeStruct(whole, F32)), 0, 2, limit
        )(normed, att_in)
        share = rows // parts
        all_keys = jax.ShapeDtypeStruct((share, n_col * cols, width), BF16)
        done = []
        for part in range(parts):
            base = part * share
            final = part == parts - 1
            keys, values = call(
                make_spread_kernel(n_col, base), (all_keys, all_keys), 0, n_col + 3, limit
            )(*others[part], key, value, gains, att_in)
            result = call(
                make_attend_kernel(n_col, n_blk, grid.place, base, len(done) * final),
                wide if final else jax.ShapeDtypeStruct((share, cols, width), BF16),
                0,
                n_blk + 7 + len(done) * final,
                limit,
                [pltpu.VMEM((H * cols, n_col * cols), F32)],
                held_out=not final,
            )(
                *biases,
                query,
                keys,
                values,
                att_gate,
                mids[part],
                live,
                att_out,
                *(done if final else []),
            )
            done.append(result)
        return result

    return body


def solution(mesh):
    grid = Grid(mesh.shape["row"], mesh.shape["col"])
    placed = (P("row", "col", None), P(), P(), P(), P(), P(), P(), P(), P(), P())
    return jax.shard_map(
        make_body(grid), mesh=mesh, in_specs=placed, out_specs=P("row", "col", None), check_vma=False
    )
```

```python
import math

import jax
import jax.numpy as jnp
from jax import lax
from jax.experimental import pallas as pl
from jax.experimental.pallas import tpu as pltpu
from jax.sharding import PartitionSpec as P


CH = 128
H = 4
DH = 32
KCD = 16
SLOT = 64

EPSILON = 1e-05
NEG_SCORE = -1e30
MIB = 1024 * 1024
RESIDENT_LIMIT = 32 * MIB

F32 = jnp.float32
BF16 = jnp.bfloat16


def layer_norm(values, norm_gain):
    centre = values - jnp.mean(values, axis=-1, keepdims=True)
    spread = jnp.mean(centre * centre, axis=-1, keepdims=True)
    return centre * lax.rsqrt(spread + EPSILON) * norm_gain


def sigmoid(values):
    return jax.nn.sigmoid(values)


def unroll_of(count, cols):
    return max(1, min(count, 1024 // cols))


def dot(a, b):
    return jnp.dot(a, b, preferred_element_type=F32)


def dot_nt(a, b):
    return lax.dot_general(a, b, (((1,), (1,)), ((), ())), preferred_element_type=F32)


def call(kernel, out_shape, n_smem, n_in, limit, scratch=(), held_out=True, aliases=None):
    smem = pl.BlockSpec(memory_space=pltpu.SMEM)
    vmem = pl.BlockSpec(memory_space=pltpu.VMEM)
    outs = jax.tree.map(lambda _: vmem, out_shape)
    resident = limit < RESIDENT_LIMIT
    if resident and held_out:
        out_shape = jax.tree.map(lambda o: pltpu.VMEM(o.shape, o.dtype), out_shape)
    run = pl.pallas_call(
        kernel,
        out_shape=out_shape,
        in_specs=[smem] * n_smem + [vmem] * n_in,
        out_specs=outs,
        scratch_shapes=list(scratch),
        input_output_aliases=aliases or {},
        compiler_params=pltpu.CompilerParams(vmem_limit_bytes=limit),
    )

    def apply(*args):
        if not resident:
            return run(*args)
        held = [pltpu.with_memory_space_constraint(a, pltpu.VMEM) for a in args[n_smem:]]
        return run(*args[:n_smem], *held)

    return apply


def make_edge_kernel(cols, n_col, col_of):
    def kernel(len_ref, pair_ref, gain_ref, sum_gain_ref, att_gain_ref, w_ref, *rest):
        left_ref, right_ref, gains_ref, live_ref, scratch_ref, group_ref, proj_ref, sems = rest
        rows, kcd, width = group_ref.shape
        group_copy = pltpu.make_async_copy(pair_ref.at[:, 0:kcd, :], group_ref, sems.at[0])
        proj_copy = pltpu.make_async_copy(w_ref.at[:, 0 : 4 * CH], proj_ref, sems.at[1])
        group_copy.start()
        proj_copy.start()
        row_start = lax.axis_index("row") * rows
        col_start = lax.axis_index("col") * cols
        cells = rows * kcd
        gains_ref[0:1, :] = sum_gain_ref[...]
        gains_ref[1:2, :] = att_gain_ref[...]
        gains_ref[2:3, :] = gain_ref[...]
        chains = cols // SLOT
        lane = lax.broadcasted_iota(jnp.int32, (1, cols), 1)
        for d in range(n_col):
            limit = jnp.zeros((1, cols), jnp.int32)
            for q in range(chains):
                length = len_ref[col_of(d) * chains + q]
                limit = jnp.where(lane // SLOT == q, q * SLOT + length, limit)
            live_ref[:, d * cols : (d + 1) * cols] = jnp.where(lane < limit, 1.0, 0.0).astype(F32)
        group_copy.wait()
        normed = layer_norm(group_ref[...].reshape(cells, width).astype(F32), gain_ref[...])
        proj_copy.wait()
        proj = dot(normed.astype(BF16), proj_ref[...])
        row_len = len_ref[row_start // SLOT]
        row_base = row_start % SLOT
        col_len = len_ref[col_start // SLOT]
        cell = lax.broadcasted_iota(jnp.int32, (cells, width), 0)
        row_live = (cell // kcd + row_base) < row_len
        live = jnp.where(row_live & (cell % kcd < col_len), 1.0, 0.0).astype(F32)
        right = sigmoid(proj[:, 2 * CH : 3 * CH]) * proj[:, 3 * CH : 4 * CH] * live
        scratch_ref[...] = right
        for k in range(kcd):
            right_ref[k] = scratch_ref[pl.ds(k, rows, stride=kcd), :].astype(BF16)
        left = sigmoid(proj[:, :CH]) * proj[:, CH : 2 * CH] * live
        left_ref[...] = left.astype(BF16).reshape(rows, kcd, width)

    return kernel


def gate_kernel(pair_ref, gains_ref, w_ref, out_ref):
    rows, cols, width = pair_ref.shape
    step = 2

    def body(t, carry):
        at = pl.ds(t * step, step)
        x = pair_ref[at].reshape(step * cols, width).astype(F32)
        normed = layer_norm(x, gains_ref[2:3, :]).astype(BF16)
        out_ref[at] = sigmoid(dot(normed, w_ref[:, 4 * CH :])).reshape(step, cols, width)
        return carry

    lax.fori_loop(0, rows // step, body, 0, unroll=unroll_of(rows // step, cols))


def add_sums(left_ref, lefts, rights, sum_ref, places):
    rows = sum_ref.shape[0]
    kcd, width = lefts[0].shape[1:]
    blk = rights[0].shape[2]
    group = 8
    for d, left in enumerate(lefts):
        left_ref[d] = left[...].reshape(rows * kcd, width).astype(F32)
    for right_ref, place in zip(rights, places):
        first = pl.multiple_of(place * blk, blk)

        def sums(g, carry, right_ref=right_ref, first=first):
            acc = [jnp.zeros((blk, width), F32) for _ in range(group)]
            for d in range(len(lefts)):
                for k in range(kcd):
                    right = right_ref[d, k].astype(F32)
                    for u in range(group):
                        left = left_ref[d, pl.ds((g * group + u) * kcd + k, 1), :]
                        acc[u] = acc[u] + left * right
            for u in range(group):
                sum_ref[g * group + u, pl.ds(first, blk), :] = acc[u]
            return carry

        lax.fori_loop(0, rows // group, sums, 0)


def make_sum_kernel(n_col, blocks, place):
    def kernel(*refs):
        lefts = refs[:n_col]
        rights = refs[n_col : n_col + len(blocks)]
        sum_ref, left_ref = refs[-2:]
        add_sums(left_ref, lefts, rights, sum_ref, [place(s) for s in blocks])

    return kernel


def make_tri_kernel(n_col, blocks, place, parts):
    def kernel(*refs):
        lefts = refs[:n_col]
        rights = refs[n_col : n_col + len(blocks)]
        pair_ref, gate_ref, gains_ref, w_ref, bias_w_ref = refs[
            n_col + len(blocks) : n_col + len(blocks) + 5
        ]
        mid_refs = refs[-5 - parts : -5]
        norm_ref, bias_ref, sum_ref, left_ref, bias_scr = refs[-5:]
        rows, cols, width = pair_ref.shape
        add_sums(left_ref, lefts, rights, sum_ref, [place(s) for s in blocks])
        step = 2

        share = rows // parts // step
        for part, mid_ref in enumerate(mid_refs):

            def finish(t, carry, part=part, mid_ref=mid_ref):
                row = part * share * step + t * step
                at = pl.ds(row, step)
                total = sum_ref[at].reshape(step * cols, width)
                normed = layer_norm(total, gains_ref[0:1, :]).astype(BF16)
                update = dot(normed, w_ref[...])
                pair = pair_ref[at].reshape(step * cols, width).astype(F32)
                gate = gate_ref[at].reshape(step * cols, width)
                mid = (pair + gate * update).astype(BF16)
                mid_ref[pl.ds(t * step, step)] = mid.reshape(step, cols, width)
                att = layer_norm(mid.astype(F32), gains_ref[1:2, :]).astype(BF16)
                norm_ref[at] = att.reshape(step, cols, width)
                bias = dot_nt(bias_w_ref[...], att)
                for u in range(step):
                    bias_scr[row + u] = bias[:, u * cols : (u + 1) * cols]
                return carry

            lax.fori_loop(0, share, finish, 0, unroll=unroll_of(share, cols))
        for h in range(H):
            bias_ref[h] = bias_scr[:, h, :].astype(BF16)

    return kernel


def project_kernel(norm_ref, w_ref, q_ref, k_ref, v_ref, gate_ref):
    rows, cols, width = norm_ref.shape
    step = 2

    def body(t, carry):
        at = pl.ds(t * step, step)
        out = dot(norm_ref[at].reshape(step * cols, width), w_ref[...])
        shape = (step, cols, width)
        q_ref[at] = out[:, :width].astype(BF16).reshape(shape)
        k_ref[at] = out[:, width : 2 * width].astype(BF16).reshape(shape)
        v_ref[at] = out[:, 2 * width : 3 * width].astype(BF16).reshape(shape)
        gate_ref[at] = sigmoid(out[:, 3 * width :]).reshape(shape)
        return carry

    lax.fori_loop(0, rows // step, body, 0, unroll=unroll_of(rows // step, cols))


def make_spread_kernel(n_col, base):
    def kernel(*refs):
        others = refs[: n_col - 1]
        k_ref, v_ref, gains_ref, kv_w_ref, keys_ref, values_ref = refs[n_col - 1 :]
        rows = keys_ref.shape[0]
        cols, width = k_ref.shape[1:]
        step = 2

        def spread(t, carry):
            at = pl.ds(t * step, step)
            own = pl.ds(base + t * step, step)
            keys_ref[at, 0:cols] = k_ref[own]
            values_ref[at, 0:cols] = v_ref[own]
            for d in range(n_col - 1):
                there = others[d][at].reshape(step * cols, width).astype(F32)
                normed = layer_norm(there, gains_ref[1:2, :]).astype(BF16)
                kv = dot(normed, kv_w_ref[:, width : 3 * width]).astype(BF16)
                low = (d + 1) * cols
                keys_ref[at, low : low + cols] = kv[:, :width].reshape(step, cols, width)
                values_ref[at, low : low + cols] = kv[:, width:].reshape(step, cols, width)
            return carry

        lax.fori_loop(0, rows // step, spread, 0, unroll=unroll_of(rows // step, cols))

    return kernel


def make_attend_kernel(n_col, n_blk, place, base, n_done):
    def kernel(*refs):
        biases = refs[:n_blk]
        q_ref, keys_ref, values_ref, gate_ref, mid_ref, live_ref, out_w_ref = refs[
            n_blk : n_blk + 7
        ]
        done = refs[n_blk + 7 : n_blk + 7 + n_done]
        whole_ref, bias_ref = refs[n_blk + 7 + n_done :]
        rows, cols, width = mid_ref.shape
        first_row = base if n_done else 0
        out_ref = whole_ref.at[first_row : first_row + rows]
        for at, done_ref in enumerate(done):
            whole_ref[at * rows : (at + 1) * rows] = done_ref[...]
        blk = biases[0].shape[2]
        for d in range(n_col):
            live = jnp.broadcast_to(live_ref[:, d * cols : (d + 1) * cols], (blk, cols)) > 0.5
            for s in range(n_blk):
                first = place(s) * blk
                for h in range(H):
                    at = pl.multiple_of(h * cols + first, blk)
                    value = biases[s][d, h].astype(F32)
                    bias_ref[pl.ds(at, blk), d * cols : (d + 1) * cols] = jnp.where(
                        live, value, NEG_SCORE
                    )
        head = lax.broadcasted_iota(jnp.int32, (cols, width), 1) // DH
        scale = 1.0 / math.sqrt(DH)
        ones = jnp.ones((n_col * cols, width), BF16)

        step = 2

        def attend(i, carry):
            key = keys_ref[i]
            value = jnp.concatenate([values_ref[i], ones], axis=1)
            query = q_ref[base + i]
            stack = jnp.concatenate(
                [jnp.where(head == h, query, jnp.zeros_like(query)) for h in range(H)], axis=0
            )
            scores = dot_nt(stack, key) * scale + bias_ref[...]
            top = jnp.max(scores, axis=-1, keepdims=True)
            weights = jnp.exp(scores - top).astype(BF16)
            both = dot(weights, value)
            summed = both[:cols, :width]
            totals = both[:cols, width:]
            for h in range(1, H):
                mine = head == h
                part = both[h * cols : (h + 1) * cols]
                summed = jnp.where(mine, part[:, :width], summed)
                totals = jnp.where(mine, part[:, width:], totals)
            out_ref[i] = (summed / totals * gate_ref[base + i]).astype(BF16)
            return carry

        lax.fori_loop(0, rows, attend, 0, unroll=max(1, min(rows, 2**18 // (cols * n_col * cols))))

        def finish(t, carry):
            at = pl.ds(t * step, step)
            attended = out_ref[at].reshape(step * cols, width)
            new = mid_ref[at].reshape(step * cols, width).astype(F32) + dot(attended, out_w_ref[...])
            out_ref[at] = new.astype(BF16).reshape(step, cols, width)
            return carry

        lax.fori_loop(0, rows // step, finish, 0, unroll=unroll_of(rows // step, cols))

    return kernel


class Grid:
    def __init__(self, n_row, n_col):
        self.n_row = n_row
        self.n_col = n_col
        self.n_blk = n_row // n_col
        self.fast = n_col == 2 and n_row & (n_row - 1) == 0
        self.offsets = [0]
        if self.fast:
            bit = self.n_blk // 2
            while bit:
                self.offsets = self.offsets + [o ^ bit for o in self.offsets]
                bit //= 2

    def groups(self):
        if not self.fast or self.n_blk < 8:
            return [], list(range(self.n_blk))
        half = self.n_blk // 2
        parts = [range(half // 2), range(half // 2, half - 1), range(half - 1, half)]
        groups = [[t for s in part for t in (s, s + half)] for part in parts]
        return groups[:-1] + [groups[-1][:1]], groups[-1][1:]

    def place(self, s):
        if self.fast:
            return (lax.axis_index("row") & (self.n_blk - 1)) ^ self.offsets[s]
        return s

    def col_of(self, d):
        return (lax.axis_index("col") + d) % self.n_col

    def move(self, value, target):
        pairs = []
        for r in range(self.n_row):
            for c in range(self.n_col):
                to = target(r, c)
                if to is not None:
                    pairs.append((r * self.n_col + c, to[0] * self.n_col + to[1]))
        return lax.ppermute(value, ("row", "col"), pairs)

    def shift_col(self, value, d):
        return self.move(value, lambda r, c: (r, (c - d) % self.n_col))

    def flip_row(self, value, bit):
        return self.move(value, lambda r, c: (r ^ bit, c))

    def gather(self, own, direct):
        if not self.fast:
            stacked = lax.all_gather(own, "row", axis=0)
            stacked = lax.all_to_all(stacked, "col", split_axis=0, concat_axis=0, tiled=True)
            stacked = stacked.reshape((self.n_col, self.n_blk) + own.shape)
            order = (lax.axis_index("col") + jnp.arange(self.n_col)) % self.n_col
            stacked = jnp.take(stacked, order, axis=0)
            return [stacked[:, s] for s in range(self.n_blk)]
        half = self.n_row // 2
        same = lax.axis_index("row") // half == lax.axis_index("col")

        def inside(r, c):
            return r // half == c

        def first(r, c):
            return (r ^ half, c) if inside(r, c) else (r, 1 - c)

        def second(r, c):
            return None if inside(r, c) else (r ^ half, 1 - c)

        near = self.move(own, first)
        far = self.move(own, second)
        pair = jnp.where(same, jnp.stack([own, near]), jnp.stack([near, far]))
        blocks = [pair]
        bit = self.n_blk // 2
        while bit:
            moved = []
            for at, block in enumerate(blocks):
                far_bits = bit ^ self.offsets[at]
                if direct and bit > 1:
                    moved.append(self.flip_row(pair, far_bits))
                else:
                    moved.append(self.flip_row(block, bit))
            blocks = blocks + moved
            bit //= 2
        return blocks


def make_body(grid):
    def body(
        pair_rep, chain_len, tri_gain, tri_in, sum_gain, tri_out, att_gain, att_in, att_bias, att_out
    ):
        rows, cols, width = pair_rep.shape
        n_col, n_blk = grid.n_col, grid.n_blk
        whole = (rows, cols, width)
        parts = 2 if grid.fast else 1
        limit = min(60 * MIB, 12 * MIB + 24 * H * cols * n_col * cols * 4)
        tri_gain = tri_gain.reshape(1, width)
        sum_gain = sum_gain.reshape(1, width)
        att_gain = att_gain.reshape(1, width)

        anywhere = pl.BlockSpec(memory_space=pl.ANY)
        small = pl.BlockSpec(memory_space=pltpu.VMEM)
        held = limit < RESIDENT_LIMIT
        shape = pltpu.VMEM if held else jax.ShapeDtypeStruct
        left, right, gains, live = pl.pallas_call(
            make_edge_kernel(cols, n_col, grid.col_of),
            name="edges",
            out_shape=(
                shape((rows, KCD, width), BF16),
                shape((KCD, rows, width), BF16),
                shape((3, width), F32),
                shape((1, n_col * cols), F32),
            ),
            in_specs=[
                pl.BlockSpec(memory_space=pltpu.SMEM),
                anywhere,
                small,
                small,
                small,
                anywhere,
            ],
            out_specs=(small, small, small, small),
            scratch_shapes=[
                pltpu.VMEM((rows * KCD, width), F32),
                pltpu.VMEM((rows, KCD, width), BF16),
                pltpu.VMEM((width, 4 * CH), BF16),
                pltpu.SemaphoreType.DMA((2,)),
            ],
        )(chain_len, pair_rep, tri_gain, sum_gain, att_gain, tri_in)
        rights = grid.gather(right, False)
        lefts = [left] + [grid.shift_col(left, d) for d in range(1, n_col)]
        gate = call(gate_kernel, jax.ShapeDtypeStruct(whole, F32), 0, 3, limit)(
            pair_rep, gains, tri_in
        )
        early, last = grid.groups()
        left_scr = pltpu.VMEM((n_col, rows * KCD, width), F32)
        sums = []
        for blocks in early:
            sums = [
                call(
                    make_sum_kernel(n_col, blocks, grid.place),
                    jax.ShapeDtypeStruct(whole, F32),
                    0,
                    n_col + len(blocks) + len(sums),
                    limit,
                    [left_scr],
                    aliases={n_col + len(blocks): 0} if sums else {},
                )(*lefts, *[rights[s] for s in blocks], *sums)
            ]
        *mids, normed, bias, _ = call(
            make_tri_kernel(n_col, last, grid.place, parts),
            (
                *[jax.ShapeDtypeStruct((rows // parts, cols, width), BF16)] * parts,
                jax.ShapeDtypeStruct(whole, BF16),
                jax.ShapeDtypeStruct((H, rows, cols), BF16),
                jax.ShapeDtypeStruct(whole, F32),
            ),
            0,
            n_col + len(last) + 5 + len(sums),
            limit,
            [left_scr, pltpu.VMEM((rows, H, cols), F32)],
            aliases={n_col + len(last) + 5: parts + 2} if sums else {},
        )(*lefts, *[rights[s] for s in last], pair_rep, gate, gains, tri_out, att_bias.T, *sums)
        biases = grid.gather(bias, True)
        others = []
        for mid in mids:
            others.append([grid.shift_col(mid, d) for d in range(1, n_col)])
        wide = jax.ShapeDtypeStruct(whole, BF16)
        query, key, value, att_gate = call(
            project_kernel, (wide, wide, wide, jax.ShapeDtypeStruct(whole, F32)), 0, 2, limit
        )(normed, att_in)
        share = rows // parts
        all_keys = jax.ShapeDtypeStruct((share, n_col * cols, width), BF16)
        done = []
        for part in range(parts):
            base = part * share
            final = part == parts - 1
            keys, values = call(
                make_spread_kernel(n_col, base), (all_keys, all_keys), 0, n_col + 3, limit
            )(*others[part], key, value, gains, att_in)
            result = call(
                make_attend_kernel(n_col, n_blk, grid.place, base, len(done) * final),
                wide if final else jax.ShapeDtypeStruct((share, cols, width), BF16),
                0,
                n_blk + 7 + len(done) * final,
                limit,
                [pltpu.VMEM((H * cols, n_col * cols), F32)],
                held_out=not final,
            )(
                *biases,
                query,
                keys,
                values,
                att_gate,
                mids[part],
                live,
                att_out,
                *(done if final else []),
            )
            done.append(result)
        return result

    return body


def solution(mesh):
    grid = Grid(mesh.shape["row"], mesh.shape["col"])
    placed = (P("row", "col", None), P(), P(), P(), P(), P(), P(), P(), P(), P())
    return jax.shard_map(
        make_body(grid), mesh=mesh, in_specs=placed, out_specs=P("row", "col", None), check_vma=False
    )
```

```python
import math

import jax
import jax.numpy as jnp
from jax import lax
from jax.experimental import pallas as pl
from jax.experimental.pallas import tpu as pltpu
from jax.sharding import PartitionSpec as P


CH = 128
H = 4
DH = 32
KCD = 16
SLOT = 64

EPSILON = 1e-05
NEG_SCORE = -1e30
MIB = 1024 * 1024
RESIDENT_LIMIT = 32 * MIB

F32 = jnp.float32
BF16 = jnp.bfloat16


def layer_norm(values, norm_gain):
    centre = values - jnp.mean(values, axis=-1, keepdims=True)
    spread = jnp.mean(centre * centre, axis=-1, keepdims=True)
    return centre * lax.rsqrt(spread + EPSILON) * norm_gain


def sigmoid(values):
    return jax.nn.sigmoid(values)


def unroll_of(count, cols):
    return max(1, min(count, 1024 // cols))


def dot(a, b):
    return jnp.dot(a, b, preferred_element_type=F32)


def dot_nt(a, b):
    return lax.dot_general(a, b, (((1,), (1,)), ((), ())), preferred_element_type=F32)


def call(kernel, out_shape, n_smem, n_in, limit, scratch=(), held_out=True, aliases=None, streamed=False):
    smem = pl.BlockSpec(memory_space=pltpu.SMEM)
    vmem = pl.BlockSpec(memory_space=pltpu.VMEM)
    place = pl.BlockSpec(memory_space=pl.ANY) if streamed else vmem
    outs = jax.tree.map(lambda _: place, out_shape)
    resident = limit < RESIDENT_LIMIT
    if resident and held_out:
        out_shape = jax.tree.map(lambda o: pltpu.VMEM(o.shape, o.dtype), out_shape)
    run = pl.pallas_call(
        kernel,
        out_shape=out_shape,
        in_specs=[smem] * n_smem + [vmem] * n_in,
        out_specs=outs,
        scratch_shapes=list(scratch),
        input_output_aliases=aliases or {},
        compiler_params=pltpu.CompilerParams(vmem_limit_bytes=limit),
    )

    def apply(*args):
        if not resident:
            return run(*args)
        held = [pltpu.with_memory_space_constraint(a, pltpu.VMEM) for a in args[n_smem:]]
        return run(*args[:n_smem], *held)

    return apply


def make_edge_kernel(cols, n_col, col_of):
    def kernel(len_ref, pair_ref, gain_ref, sum_gain_ref, att_gain_ref, w_ref, *rest):
        left_ref, right_ref, gains_ref, live_ref, scratch_ref, group_ref, proj_ref, sems = rest
        rows, kcd, width = group_ref.shape
        group_copy = pltpu.make_async_copy(pair_ref.at[:, 0:kcd, :], group_ref, sems.at[0])
        proj_copy = pltpu.make_async_copy(w_ref.at[:, 0 : 4 * CH], proj_ref, sems.at[1])
        group_copy.start()
        proj_copy.start()
        row_start = lax.axis_index("row") * rows
        col_start = lax.axis_index("col") * cols
        cells = rows * kcd
        gains_ref[0:1, :] = sum_gain_ref[...]
        gains_ref[1:2, :] = att_gain_ref[...]
        gains_ref[2:3, :] = gain_ref[...]
        chains = cols // SLOT
        lane = lax.broadcasted_iota(jnp.int32, (1, cols), 1)
        for d in range(n_col):
            limit = jnp.zeros((1, cols), jnp.int32)
            for q in range(chains):
                length = len_ref[col_of(d) * chains + q]
                limit = jnp.where(lane // SLOT == q, q * SLOT + length, limit)
            live_ref[:, d * cols : (d + 1) * cols] = jnp.where(lane < limit, 1.0, 0.0).astype(F32)
        group_copy.wait()
        normed = layer_norm(group_ref[...].reshape(cells, width).astype(F32), gain_ref[...])
        proj_copy.wait()
        proj = dot(normed.astype(BF16), proj_ref[...])
        row_len = len_ref[row_start // SLOT]
        row_base = row_start % SLOT
        col_len = len_ref[col_start // SLOT]
        cell = lax.broadcasted_iota(jnp.int32, (cells, width), 0)
        row_live = (cell // kcd + row_base) < row_len
        live = jnp.where(row_live & (cell % kcd < col_len), 1.0, 0.0).astype(F32)
        right = sigmoid(proj[:, 2 * CH : 3 * CH]) * proj[:, 3 * CH : 4 * CH] * live
        scratch_ref[...] = right
        for k in range(kcd):
            right_ref[k] = scratch_ref[pl.ds(k, rows, stride=kcd), :].astype(BF16)
        left = sigmoid(proj[:, :CH]) * proj[:, CH : 2 * CH] * live
        left_ref[...] = left.astype(BF16).reshape(rows, kcd, width)

    return kernel


def gate_kernel(pair_ref, gains_ref, w_ref, out_ref):
    rows, cols, width = pair_ref.shape
    step = 2

    def body(t, carry):
        at = pl.ds(t * step, step)
        x = pair_ref[at].reshape(step * cols, width).astype(F32)
        normed = layer_norm(x, gains_ref[2:3, :]).astype(BF16)
        out_ref[at] = sigmoid(dot(normed, w_ref[:, 4 * CH :])).reshape(step, cols, width)
        return carry

    lax.fori_loop(0, rows // step, body, 0, unroll=unroll_of(rows // step, cols))


def add_sums(left_ref, lefts, rights, sum_ref, places):
    rows = sum_ref.shape[0]
    kcd, width = lefts[0].shape[1:]
    blk = rights[0].shape[2]
    group = 8
    for d, left in enumerate(lefts):
        left_ref[d] = left[...].reshape(rows * kcd, width).astype(F32)
    for right_ref, place in zip(rights, places):
        first = pl.multiple_of(place * blk, blk)

        def sums(g, carry, right_ref=right_ref, first=first):
            acc = [jnp.zeros((blk, width), F32) for _ in range(group)]
            for d in range(len(lefts)):
                for k in range(kcd):
                    right = right_ref[d, k].astype(F32)
                    for u in range(group):
                        left = left_ref[d, pl.ds((g * group + u) * kcd + k, 1), :]
                        acc[u] = acc[u] + left * right
            for u in range(group):
                sum_ref[g * group + u, pl.ds(first, blk), :] = acc[u]
            return carry

        lax.fori_loop(0, rows // group, sums, 0)


def make_sum_kernel(n_col, blocks, place):
    def kernel(*refs):
        lefts = refs[:n_col]
        rights = refs[n_col : n_col + len(blocks)]
        sum_ref, left_ref = refs[-2:]
        add_sums(left_ref, lefts, rights, sum_ref, [place(s) for s in blocks])

    return kernel


def make_tri_kernel(n_col, blocks, place, parts):
    def kernel(*refs):
        lefts = refs[:n_col]
        rights = refs[n_col : n_col + len(blocks)]
        pair_ref, gate_ref, gains_ref, w_ref, bias_w_ref = refs[
            n_col + len(blocks) : n_col + len(blocks) + 5
        ]
        mid_refs = refs[-5 - parts : -5]
        norm_ref, bias_ref, sum_ref, left_ref, bias_scr = refs[-5:]
        rows, cols, width = pair_ref.shape
        add_sums(left_ref, lefts, rights, sum_ref, [place(s) for s in blocks])
        step = 2

        share = rows // parts // step
        for part, mid_ref in enumerate(mid_refs):

            def finish(t, carry, part=part, mid_ref=mid_ref):
                row = part * share * step + t * step
                at = pl.ds(row, step)
                total = sum_ref[at].reshape(step * cols, width)
                normed = layer_norm(total, gains_ref[0:1, :]).astype(BF16)
                update = dot(normed, w_ref[...])
                pair = pair_ref[at].reshape(step * cols, width).astype(F32)
                gate = gate_ref[at].reshape(step * cols, width)
                mid = (pair + gate * update).astype(BF16)
                mid_ref[pl.ds(t * step, step)] = mid.reshape(step, cols, width)
                att = layer_norm(mid.astype(F32), gains_ref[1:2, :]).astype(BF16)
                norm_ref[at] = att.reshape(step, cols, width)
                bias = dot_nt(bias_w_ref[...], att)
                for u in range(step):
                    bias_scr[row + u] = bias[:, u * cols : (u + 1) * cols]
                return carry

            lax.fori_loop(0, share, finish, 0, unroll=unroll_of(share, cols))
        for h in range(H):
            bias_ref[h] = bias_scr[:, h, :].astype(BF16)

    return kernel


def project_kernel(norm_ref, w_ref, q_ref, k_ref, v_ref, gate_ref):
    rows, cols, width = norm_ref.shape
    step = 2

    def body(t, carry):
        at = pl.ds(t * step, step)
        out = dot(norm_ref[at].reshape(step * cols, width), w_ref[...])
        shape = (step, cols, width)
        q_ref[at] = out[:, :width].astype(BF16).reshape(shape)
        k_ref[at] = out[:, width : 2 * width].astype(BF16).reshape(shape)
        v_ref[at] = out[:, 2 * width : 3 * width].astype(BF16).reshape(shape)
        gate_ref[at] = sigmoid(out[:, 3 * width :]).reshape(shape)
        return carry

    lax.fori_loop(0, rows // step, body, 0, unroll=unroll_of(rows // step, cols))


def make_spread_kernel(n_col, base):
    def kernel(*refs):
        others = refs[: n_col - 1]
        k_ref, v_ref, gains_ref, kv_w_ref, keys_ref, values_ref = refs[n_col - 1 :]
        rows = keys_ref.shape[0]
        cols, width = k_ref.shape[1:]
        step = 2

        def spread(t, carry):
            at = pl.ds(t * step, step)
            own = pl.ds(base + t * step, step)
            keys_ref[at, 0:cols] = k_ref[own]
            values_ref[at, 0:cols] = v_ref[own]
            for d in range(n_col - 1):
                there = others[d][at].reshape(step * cols, width).astype(F32)
                normed = layer_norm(there, gains_ref[1:2, :]).astype(BF16)
                kv = dot(normed, kv_w_ref[:, width : 3 * width]).astype(BF16)
                low = (d + 1) * cols
                keys_ref[at, low : low + cols] = kv[:, :width].reshape(step, cols, width)
                values_ref[at, low : low + cols] = kv[:, width:].reshape(step, cols, width)
            return carry

        lax.fori_loop(0, rows // step, spread, 0, unroll=unroll_of(rows // step, cols))

    return kernel


def make_attend_kernel(n_col, n_blk, place, base, n_done, stream):
    def kernel(*refs):
        biases = refs[:n_blk]
        q_ref, keys_ref, values_ref, gate_ref, mid_ref, live_ref, out_w_ref = refs[
            n_blk : n_blk + 7
        ]
        done = refs[n_blk + 7 : n_blk + 7 + n_done]
        rows, cols, width = mid_ref.shape
        if stream:
            bias_ref, whole_ref, out_ref, sems = refs[n_blk + 7 + n_done :]
        else:
            out_ref, bias_ref = refs[n_blk + 7 + n_done :]
        copies = []
        for at, done_ref in enumerate(done):
            copies.append(
                pltpu.make_async_copy(
                    done_ref, whole_ref.at[at * rows : (at + 1) * rows], sems.at[at]
                )
            )
            copies[-1].start()
        for d in range(n_col if n_blk else 0):
            blk = biases[0].shape[2]
            live = jnp.broadcast_to(live_ref[:, d * cols : (d + 1) * cols], (blk, cols)) > 0.5
            for s in range(n_blk):
                first = place(s) * blk
                for h in range(H):
                    at = pl.multiple_of(h * cols + first, blk)
                    value = biases[s][d, h].astype(F32)
                    bias_ref[pl.ds(at, blk), d * cols : (d + 1) * cols] = jnp.where(
                        live, value, NEG_SCORE
                    )
        head = lax.broadcasted_iota(jnp.int32, (cols, width), 1) // DH
        scale = 1.0 / math.sqrt(DH)
        ones = jnp.ones((n_col * cols, width), BF16)

        step = 2

        def attend(i, carry):
            key = keys_ref[i]
            value = jnp.concatenate([values_ref[i], ones], axis=1)
            query = q_ref[base + i]
            stack = jnp.concatenate(
                [jnp.where(head == h, query, jnp.zeros_like(query)) for h in range(H)], axis=0
            )
            scores = dot_nt(stack, key) * scale + bias_ref[...]
            top = jnp.max(scores, axis=-1, keepdims=True)
            weights = jnp.exp(scores - top).astype(BF16)
            both = dot(weights, value)
            summed = both[:cols, :width]
            totals = both[:cols, width:]
            for h in range(1, H):
                mine = head == h
                part = both[h * cols : (h + 1) * cols]
                summed = jnp.where(mine, part[:, :width], summed)
                totals = jnp.where(mine, part[:, width:], totals)
            out_ref[i] = (summed / totals * gate_ref[base + i]).astype(BF16)
            return carry

        lax.fori_loop(0, rows, attend, 0, unroll=max(1, min(rows, 2**18 // (cols * n_col * cols))))

        def finish(t):
            at = pl.ds(t * step, step)
            attended = out_ref[at].reshape(step * cols, width)
            new = mid_ref[at].reshape(step * cols, width).astype(F32) + dot(attended, out_w_ref[...])
            out_ref[at] = new.astype(BF16).reshape(step, cols, width)

        if not stream:
            lax.fori_loop(
                0,
                rows // step,
                lambda t, carry: (finish(t), carry)[1],
                0,
                unroll=unroll_of(rows // step, cols),
            )
            return
        for t in range(rows // step):
            finish(t)
            copies.append(
                pltpu.make_async_copy(
                    out_ref.at[t * step : (t + 1) * step],
                    whole_ref.at[base + t * step : base + (t + 1) * step],
                    sems.at[n_done + t],
                )
            )
            copies[-1].start()
        for copy in copies:
            copy.wait()

    return kernel


class Grid:
    def __init__(self, n_row, n_col):
        self.n_row = n_row
        self.n_col = n_col
        self.n_blk = n_row // n_col
        self.fast = n_col == 2 and n_row & (n_row - 1) == 0
        self.offsets = [0]
        if self.fast:
            bit = self.n_blk // 2
            while bit:
                self.offsets = self.offsets + [o ^ bit for o in self.offsets]
                bit //= 2

    def groups(self):
        if not self.fast or self.n_blk < 8:
            return [], list(range(self.n_blk))
        half = self.n_blk // 2
        parts = [range(half // 2), range(half // 2, half - 1), range(half - 1, half)]
        groups = [[t for s in part for t in (s, s + half)] for part in parts]
        return groups[:-1] + [groups[-1][:1]], groups[-1][1:]

    def place(self, s):
        if self.fast:
            return (lax.axis_index("row") & (self.n_blk - 1)) ^ self.offsets[s]
        return s

    def col_of(self, d):
        return (lax.axis_index("col") + d) % self.n_col

    def move(self, value, target):
        pairs = []
        for r in range(self.n_row):
            for c in range(self.n_col):
                to = target(r, c)
                if to is not None:
                    pairs.append((r * self.n_col + c, to[0] * self.n_col + to[1]))
        return lax.ppermute(value, ("row", "col"), pairs)

    def shift_col(self, value, d):
        return self.move(value, lambda r, c: (r, (c - d) % self.n_col))

    def flip_row(self, value, bit):
        return self.move(value, lambda r, c: (r ^ bit, c))

    def gather(self, own, direct):
        if not self.fast:
            stacked = lax.all_gather(own, "row", axis=0)
            stacked = lax.all_to_all(stacked, "col", split_axis=0, concat_axis=0, tiled=True)
            stacked = stacked.reshape((self.n_col, self.n_blk) + own.shape)
            order = (lax.axis_index("col") + jnp.arange(self.n_col)) % self.n_col
            stacked = jnp.take(stacked, order, axis=0)
            return [stacked[:, s] for s in range(self.n_blk)]
        half = self.n_row // 2
        same = lax.axis_index("row") // half == lax.axis_index("col")

        def inside(r, c):
            return r // half == c

        def first(r, c):
            return (r ^ half, c) if inside(r, c) else (r, 1 - c)

        def second(r, c):
            return None if inside(r, c) else (r ^ half, 1 - c)

        near = self.move(own, first)
        far = self.move(own, second)
        pair = jnp.where(same, jnp.stack([own, near]), jnp.stack([near, far]))
        blocks = [pair]
        bit = self.n_blk // 2
        while bit:
            moved = []
            for at, block in enumerate(blocks):
                far_bits = bit ^ self.offsets[at]
                if direct and bit > 1:
                    moved.append(self.flip_row(pair, far_bits))
                else:
                    moved.append(self.flip_row(block, bit))
            blocks = blocks + moved
            bit //= 2
        return blocks


def make_body(grid):
    def body(
        pair_rep, chain_len, tri_gain, tri_in, sum_gain, tri_out, att_gain, att_in, att_bias, att_out
    ):
        rows, cols, width = pair_rep.shape
        n_col = grid.n_col
        whole = (rows, cols, width)
        parts = 2 if grid.fast else 1
        limit = min(60 * MIB, 12 * MIB + 24 * H * cols * n_col * cols * 4)
        tri_gain = tri_gain.reshape(1, width)
        sum_gain = sum_gain.reshape(1, width)
        att_gain = att_gain.reshape(1, width)

        anywhere = pl.BlockSpec(memory_space=pl.ANY)
        small = pl.BlockSpec(memory_space=pltpu.VMEM)
        held = limit < RESIDENT_LIMIT
        shape = pltpu.VMEM if held else jax.ShapeDtypeStruct
        left, right, gains, live = pl.pallas_call(
            make_edge_kernel(cols, n_col, grid.col_of),
            name="edges",
            out_shape=(
                shape((rows, KCD, width), BF16),
                shape((KCD, rows, width), BF16),
                shape((3, width), F32),
                shape((1, n_col * cols), F32),
            ),
            in_specs=[
                pl.BlockSpec(memory_space=pltpu.SMEM),
                anywhere,
                small,
                small,
                small,
                anywhere,
            ],
            out_specs=(small, small, small, small),
            scratch_shapes=[
                pltpu.VMEM((rows * KCD, width), F32),
                pltpu.VMEM((rows, KCD, width), BF16),
                pltpu.VMEM((width, 4 * CH), BF16),
                pltpu.SemaphoreType.DMA((2,)),
            ],
        )(chain_len, pair_rep, tri_gain, sum_gain, att_gain, tri_in)
        rights = grid.gather(right, False)
        lefts = [left] + [grid.shift_col(left, d) for d in range(1, n_col)]
        gate = call(gate_kernel, jax.ShapeDtypeStruct(whole, F32), 0, 3, limit)(
            pair_rep, gains, tri_in
        )
        early, last = grid.groups()
        left_scr = pltpu.VMEM((n_col, rows * KCD, width), F32)
        sums = []
        for blocks in early:
            sums = [
                call(
                    make_sum_kernel(n_col, blocks, grid.place),
                    jax.ShapeDtypeStruct(whole, F32),
                    0,
                    n_col + len(blocks) + len(sums),
                    limit,
                    [left_scr],
                    aliases={n_col + len(blocks): 0} if sums else {},
                )(*lefts, *[rights[s] for s in blocks], *sums)
            ]
        *mids, normed, bias, _ = call(
            make_tri_kernel(n_col, last, grid.place, parts),
            (
                *[jax.ShapeDtypeStruct((rows // parts, cols, width), BF16)] * parts,
                jax.ShapeDtypeStruct(whole, BF16),
                jax.ShapeDtypeStruct((H, rows, cols), BF16),
                jax.ShapeDtypeStruct(whole, F32),
            ),
            0,
            n_col + len(last) + 5 + len(sums),
            limit,
            [left_scr, pltpu.VMEM((rows, H, cols), F32)],
            aliases={n_col + len(last) + 5: parts + 2} if sums else {},
        )(*lefts, *[rights[s] for s in last], pair_rep, gate, gains, tri_out, att_bias.T, *sums)
        biases = grid.gather(bias, True)
        others = []
        for mid in mids:
            others.append([grid.shift_col(mid, d) for d in range(1, n_col)])
        wide = jax.ShapeDtypeStruct(whole, BF16)
        query, key, value, att_gate = call(
            project_kernel, (wide, wide, wide, jax.ShapeDtypeStruct(whole, F32)), 0, 2, limit
        )(normed, att_in)
        share = rows // parts
        all_keys = jax.ShapeDtypeStruct((share, n_col * cols, width), BF16)
        done = []
        for part in range(parts):
            base = part * share
            final = part == parts - 1
            keys, values = call(
                make_spread_kernel(n_col, base), (all_keys, all_keys), 0, n_col + 3, limit
            )(*others[part], key, value, gains, att_in)
            stream = part > 0
            blocks = [] if stream else biases
            part_shape = jax.ShapeDtypeStruct((share, cols, width), BF16)
            bias_shape = jax.ShapeDtypeStruct((H * cols, n_col * cols), F32)
            operands = [*blocks, query, keys, values, att_gate, mids[part], live, att_out]
            if stream:
                operands += [*done, bias_all]
            result = call(
                make_attend_kernel(
                    n_col, len(blocks), grid.place, base, len(done), stream
                ),
                wide if stream else (part_shape, bias_shape),
                0,
                len(operands),
                limit,
                [
                    pltpu.VMEM((share, cols, width), BF16),
                    pltpu.SemaphoreType.DMA((len(done) + share // 2,)),
                ]
                if stream
                else [],
                held_out=not final,
                streamed=stream,
            )(*operands)
            if not stream:
                result, bias_all = result
            done.append(result)
        return result

    return body


def solution(mesh):
    grid = Grid(mesh.shape["row"], mesh.shape["col"])
    placed = (P("row", "col", None), P(), P(), P(), P(), P(), P(), P(), P(), P())
    return jax.shard_map(
        make_body(grid), mesh=mesh, in_specs=placed, out_specs=P("row", "col", None), check_vma=False
    )
```
